32 devices in a mesh: section: 4 (over z), hidden: 4 (over y, core), tok: 2 (over x).
Axes of the slice: x: 2, y: 2, z: 4, core: 2. Of those that a mesh axis runs over, the one named last changes fastest.
Arguments:
- section_inputs: bfloat16 [4, 768, 16384], P('section', 'tok', 'hidden'), may hold values from -6 to 6
- top_adjoint: bfloat16 [768, 16384], P('tok', 'hidden'), may hold values from -6 to 6
- right_first: bfloat16 [4, 128, 128, 128], P('section', ('hidden', 'tok')), may hold values from -0.5 to 0.5
- left_first: bfloat16 [4, 128, 128, 128], P('section', ('hidden', 'tok')), may hold values from -0.5 to 0.5
- right_second: bfloat16 [4, 128, 128, 128], P('section', ('hidden', 'tok')), may hold values from -0.5 to 0.5
- left_second: bfloat16 [4, 128, 128, 128], P('section', ('hidden', 'tok')), may hold values from -0.5 to 0.5
Outputs:
- input_adjoint: bfloat16 [4, 768, 16384], P('section', 'tok', 'hidden')
- grad_right_first: float32 [4, 128, 128, 128], P('section', ('hidden', 'tok'))
- grad_left_first: float32 [4, 128, 128, 128], P('section', ('hidden', 'tok'))
- grad_right_second: float32 [4, 128, 128, 128], P('section', ('hidden', 'tok'))
- grad_left_second: float32 [4, 128, 128, 128], P('section', ('hidden', 'tok'))
The draws below stay inside these ranges and needn't reach their ends.
All inputs are finite; a program needn't handle non-finite values.
Results may differ from the reference program's by a relative error of at most 0.02.
Values may be sent and summed in bfloat16 or wider, within the bound.
No kernel may reach another device: no remote copies, remote signals or barrier semaphores. Data moves between devices by JAX's collectives and lax.ppermute only.
A program may use at most 64 MiB of HBM per device.

```python
import math
import jax
import jax.numpy as jnp

BLK = 128
D = 16384
TOKENS = 768
N_SECTION = 4


def block_scale(key, dims, cuts, smallest, high):
    def one(position, parts):
        heights = jax.random.uniform(jax.random.fold_in(jax.random.fold_in(key, 6), position), (parts,), jnp.float32, smallest / len(cuts), high / len(cuts))
        return jnp.repeat(jnp.exp(heights), dims[position] // parts).reshape((-1,) + (1,) * (len(dims) - position - 1))

    gain = one(*cuts[0])
    for cut in cuts[1:]:
        gain = gain * one(*cut)
    return gain


def scatter_about(key, shape, spread, bound, shards=(), dtype=jnp.bfloat16):
    values = spread * jax.random.normal(key, shape, jnp.float32)
    if shards:
        values = values * block_scale(key, shape, shards, -0.22, 0.18)
    return jnp.clip(values, -bound, bound).astype(dtype)


def setup_inputs(seed: int = 0) -> dict:
    splits = jax.random.split(jax.random.key(seed), 7)
    return {
        "section_inputs": scatter_about(splits[0], (N_SECTION, TOKENS, D), 1.0, 6.0, ((0, 4), (1, 2), (2, 4))),
        "top_adjoint": scatter_about(splits[1], (TOKENS, D), 1.0, 6.0, ((0, 2), (1, 4))),
        "right_first": scatter_about(splits[2], (N_SECTION, BLK, BLK, BLK), BLK ** -0.5, 0.5, ((0, 4), (1, 8))),
        "left_first": scatter_about(splits[3], (N_SECTION, BLK, BLK, BLK), BLK ** -0.5, 0.5, ((0, 4), (1, 8))),
        "right_second": scatter_about(splits[4], (N_SECTION, BLK, BLK, BLK), BLK ** -0.5, 0.5, ((0, 4), (1, 8))),
        "left_second": scatter_about(splits[5], (N_SECTION, BLK, BLK, BLK), BLK ** -0.5, 0.5, ((0, 4), (1, 8))),
    }


gelu_coef = 0.7978845608028654

def gelu_parts(preact):
    inner_arg = gelu_coef * (preact + 0.044715 * preact * preact * preact)
    squashed = jnp.tanh(inner_arg)
    activation = 0.5 * preact * (1.0 + squashed)
    derivative = 0.5 * (1.0 + squashed) + 0.5 * preact * (1.0 - squashed * squashed) * gelu_coef * (1.0 + 3.0 * 0.044715 * preact * preact)
    return (activation, derivative)

def as_float(array):
    return array.astype(jnp.float32)

def reference(section_inputs, top_adjoint, right_first, left_first, right_second, left_second):
    grad_scale = 1.0 / math.sqrt(TOKENS)
    upstream = top_adjoint.reshape(TOKENS, BLK, BLK)
    adjoint_list = []
    list_right_first = []
    list_left_first = []
    list_right_second = []
    list_left_second = []
    for section_id in range(N_SECTION - 1, -1, -1):
        inputs = section_inputs[section_id].reshape(TOKENS, BLK, BLK)
        weight_rf = as_float(right_first[section_id])
        weight_lf = as_float(left_first[section_id])
        weight_rs = as_float(right_second[section_id])
        weight_ls = as_float(left_second[section_id])
        first_mid = jnp.einsum('tbi,bji->tbj', as_float(inputs), weight_rf).astype(jnp.bfloat16)
        first_out = jnp.einsum('tbj,jkb->tjk', as_float(first_mid), weight_lf)
        activation, derivative = gelu_parts(first_out)
        activation = activation.astype(jnp.bfloat16)
        second_mid = jnp.einsum('tbi,bji->tbj', as_float(activation), weight_rs).astype(jnp.bfloat16)
        upstream_f = as_float(upstream)
        grad_ls = grad_scale * jnp.einsum('tjk,tbj->jkb', upstream_f, as_float(second_mid))
        grad_mid_second = jnp.einsum('tjk,jkb->tbj', upstream_f, weight_ls).astype(jnp.bfloat16)
        grad_rs = grad_scale * jnp.einsum('tbj,tbi->bji', as_float(grad_mid_second), as_float(activation))
        grad_activation = jnp.einsum('tbj,bji->tbi', as_float(grad_mid_second), weight_rs)
        grad_pre = (grad_activation * derivative).astype(jnp.bfloat16)
        grad_lf = grad_scale * jnp.einsum('tjk,tbj->jkb', as_float(grad_pre), as_float(first_mid))
        grad_mid_first = jnp.einsum('tjk,jkb->tbj', as_float(grad_pre), weight_lf).astype(jnp.bfloat16)
        grad_rf = grad_scale * jnp.einsum('tbj,tbi->bji', as_float(grad_mid_first), as_float(inputs))
        grad_input = jnp.einsum('tbj,bji->tbi', as_float(grad_mid_first), weight_rf)
        adjoint = (upstream_f + grad_input).astype(jnp.bfloat16)
        adjoint_list.append(adjoint.reshape(TOKENS, D))
        list_right_first.append(grad_rf)
        list_left_first.append(grad_lf)
        list_right_second.append(grad_rs)
        list_left_second.append(grad_ls)
        upstream = adjoint
    input_adjoint = jnp.stack(adjoint_list[::-1], axis=0)
    return (input_adjoint, jnp.stack(list_right_first[::-1], axis=0), jnp.stack(list_left_first[::-1], axis=0), jnp.stack(list_right_second[::-1], axis=0), jnp.stack(list_left_second[::-1], axis=0))
```

```python
import functools
import math

import jax
import jax.numpy as jnp
from jax import lax
from jax.experimental import pallas as pl
from jax.experimental.pallas import tpu as pltpu
from jax.sharding import PartitionSpec as P

GROUPS = 2
SKEW = 2
UNROLL = 2


gelu_coef = 0.7978845608028654
NT = (((1,), (1,)), ((), ()))
NN = (((1,), (0,)), ((), ()))


def gelu_parts(preact):
    inner_arg = gelu_coef * (preact + 0.044715 * preact * preact * preact)
    squashed = jnp.tanh(inner_arg)
    activation = 0.5 * preact * (1.0 + squashed)
    derivative = 0.5 * (1.0 + squashed) + 0.5 * preact * (1.0 - squashed * squashed) * gelu_coef * (
        1.0 + 3.0 * 0.044715 * preact * preact
    )
    return (activation, derivative)


def dot(a, b, dims=NN):
    return lax.dot_general(a, b, dims, preferred_element_type=jnp.float32)


def partner(me, distance, count):
    if count & (count - 1) == 0:
        return me ^ distance
    return lax.rem(me + distance, count)


def source(me, distance, count):
    if count & (count - 1) == 0:
        return me ^ distance
    return lax.rem(me + count - distance, count)


def exchange(pieces, axis):
    count = len(pieces)
    out = [pieces[0]]
    for distance in range(1, count):
        if count & (count - 1) == 0:
            route = [(i, i ^ distance) for i in range(count)]
        else:
            route = [(i, (i + distance) % count) for i in range(count)]
        out.append(lax.ppermute(pieces[distance], axis, route))
    return out


class Shape:
    def __init__(self, hidden_count, token_count, local_count, block, tok_rows):
        self.hidden = hidden_count
        self.tok = token_count
        self.local = local_count
        self.block = block
        self.groups = GROUPS
        self.pairs = local_count // GROUPS
        self.tokens = block // GROUPS
        self.micro = tok_rows // self.tokens
        self.share = local_count // token_count
        self.rows = self.pairs * block
        self.picked = block // GROUPS
        self.piece = self.pairs * local_count
        self.tok_rows = tok_rows
        self.width = local_count * block


def lane_group(z, rows):
    return lax.broadcasted_iota(jnp.int32, (rows, z.block), 1) // z.tokens


def pick(parts, group):
    out = parts[0]
    for g in range(1, len(parts)):
        out = jnp.where(group == g, parts[g], out)
    return out


def spread(z, values):
    turned = [values] + [
        pltpu.roll(values, s * z.tokens, 1) for s in range(1, z.groups)
    ]
    group = lane_group(z, values.shape[0])
    return [
        pick([turned[(q - g) % z.groups] for q in range(z.groups)], group).astype(jnp.bfloat16)
        for g in range(z.groups)
    ]


def produce(z, wire, weight, values, index):
    full = dot(weight, values)
    parts = [full[g * z.picked : (g + 1) * z.picked] for g in range(z.groups)]
    wire[pl.ds(index, z.picked, stride=z.local), :] = pick(parts, lane_group(z, z.picked))


def send_pieces(z, wire, hid, piece_refs):
    for d, ref in enumerate(piece_refs):
        start = pl.multiple_of(partner(hid, d, z.hidden) * z.piece, z.piece)
        ref[...] = wire[pl.ds(start, z.piece), :].astype(jnp.bfloat16)


def block_rows(z, ref, index):
    return ref[pl.ds(pl.multiple_of(index * z.block, z.block), z.block), :]


def pair_rows(z, pair):
    return pl.ds(pl.multiple_of(pair * z.block, z.block), z.block)


def place(z, piece_refs, hid, pair, ref):
    for d, piece in enumerate(piece_refs):
        src = source(hid, d, z.hidden)
        start = pl.multiple_of(pair * z.block + src * z.local, z.local)
        ref[pl.ds(start, z.local), :] = piece[
            pl.ds(pl.multiple_of(pair * z.local, z.local), z.local), :
        ]


def consume(z, weight_ref, values, pair):
    parts = [dot(block_rows(z, weight_ref, g * z.pairs + pair), values) for g in range(z.groups)]
    return pick(parts, lane_group(z, z.block))


def loop(count, body, unroll=UNROLL):
    def step(i, carry):
        body(i)
        return carry

    lax.fori_loop(0, count, step, 0, unroll=unroll)


def whole(shape):
    return pl.BlockSpec(shape, lambda i, s: tuple(0 for _ in shape))


ANY = pl.BlockSpec(memory_space=pl.ANY)


def call(body, name, scalars, args, in_specs, outs, out_specs, scratch=(), aliases=None, flops=0):
    size = lambda a: math.prod(a.shape) * a.dtype.itemsize
    moved = sum(size(a) for a, s in zip(args, in_specs) if s.block_shape is not None)
    moved += sum(size(o) for o in outs if o.shape[0] < 10**9)
    return pl.pallas_call(
        body,
        name=name,
        grid_spec=pltpu.PrefetchScalarGridSpec(
            num_scalar_prefetch=1,
            grid=(1,),
            in_specs=in_specs,
            out_specs=out_specs,
            scratch_shapes=list(scratch),
        ),
        out_shape=outs,
        input_output_aliases=aliases or {},
        cost_estimate=pl.CostEstimate(flops=flops, bytes_accessed=moved, transcendentals=0),
        compiler_params=pltpu.CompilerParams(vmem_limit_bytes=40 * 2**20),
    )(scalars, *args)


def bf16(*shape):
    return jax.ShapeDtypeStruct(shape, jnp.bfloat16)


def f32(*shape):
    return jax.ShapeDtypeStruct(shape, jnp.float32)


def shuffle_matrix(z):
    row = lax.broadcasted_iota(jnp.int32, (z.block, z.block), 0)
    col = lax.broadcasted_iota(jnp.int32, (z.block, z.block), 1)
    g = row // z.picked
    rest = row - g * z.picked
    h = rest // z.pairs
    pair = rest - h * z.pairs
    return (col == h * z.local + g * z.pairs + pair).astype(jnp.bfloat16)


def unit_matrix(z):
    row = lax.broadcasted_iota(jnp.int32, (z.block, z.block), 0)
    col = lax.broadcasted_iota(jnp.int32, (z.block, z.block), 1)
    return (col == row).astype(jnp.bfloat16)


def prepare(z, scalars, pieces, forms):
    def body(s, *refs):
        ins, outs = refs[: z.tok], refs[z.tok :]
        unit, shuffle = unit_matrix(z), shuffle_matrix(z)
        for d, piece in enumerate(ins):
            first = source(s[3], d, z.tok) * z.share

            def one(i):
                w = block_rows(z, piece, i)
                at = pair_rows(z, first + i)
                for form, out in zip(forms, outs):
                    if form == "n":
                        out[at, :] = w
                    else:
                        left = shuffle if "p" in form else unit
                        out[at, :] = dot(left, w, NT if "t" in form else NN).astype(jnp.bfloat16)

            loop(z.share, one)

    size = z.local * z.block
    return call(
        body, "prepare", scalars, pieces,
        [whole((z.share * z.block, z.block))] * z.tok,
        [bf16(size, z.block)] * len(forms), [whole((size, z.block))] * len(forms),
    )


def piece_specs(z):
    return [whole((z.piece, z.block))] * z.hidden


def piece_shapes(z):
    return [bf16(z.piece, z.block)] * z.hidden


def wire_scratch(z):
    return pltpu.VMEM((z.picked * z.local, z.block), jnp.float32)


def matmul_flops(z, count):
    return 2 * count * z.local * z.block**3


def first_mid(z, scalars, m, inputs, weight):
    def body(s, x, w, *rest):
        pieces, wire = rest[: z.hidden], rest[z.hidden]

        def one(b):
            cols = pl.ds(pl.multiple_of(b * z.block, z.block), z.block)
            xb = x[:, cols]
            values = jnp.concatenate([xb] * z.groups, axis=0)
            full = dot(block_rows(z, w, b), values, NT)
            parts = [full[g * z.picked : (g + 1) * z.picked] for g in range(z.groups)]
            wire[pl.ds(b, z.picked, stride=z.local), :] = pick(parts, lane_group(z, z.picked))

        loop(z.local, one)
        send_pieces(z, wire, s[0], pieces)

    return call(
        body, "first_mid", scalars, [inputs, weight],
        [pl.BlockSpec((z.tokens, z.width), lambda i, s: (m, 0)), whole(weight.shape)],
        piece_shapes(z), piece_specs(z), [wire_scratch(z)], flops=matmul_flops(z, 1),
    )


def forward_wide(z, scalars, pieces, weight):
    def body(s, *refs):
        ins, w = refs[: z.hidden], refs[z.hidden]
        fw, act, deriv = refs[z.hidden + 1 :]

        def one(pair):
            place(z, ins, s[0], pair, fw)
            at = pair_rows(z, pair)
            a, d = gelu_parts(consume(z, w, fw[at, :], pair))
            act[at, :] = a.astype(jnp.bfloat16)
            deriv[at, :] = d.astype(jnp.bfloat16)

        loop(z.pairs, one)

    return call(
        body, "forward_wide", scalars, [*pieces, weight],
        piece_specs(z) + [whole(weight.shape)],
        [bf16(z.rows, z.block)] * 3, [whole((z.rows, z.block))] * 3, flops=matmul_flops(z, 1),
    )


def second_mid(z, scalars, act, weight):
    def body(s, a, w, *rest):
        pieces, wire = rest[: z.hidden], rest[z.hidden]

        def one(pair):
            values = a[pair_rows(z, pair), :].astype(jnp.float32)
            for g, repeated in enumerate(spread(z, values)):
                index = g * z.pairs + pair
                produce(z, wire, block_rows(z, w, index), repeated, index)

        loop(z.pairs, one)
        send_pieces(z, wire, s[0], pieces)

    return call(
        body, "second_mid", scalars, [act, weight],
        [whole(act.shape), whole(weight.shape)],
        piece_shapes(z), piece_specs(z), [wire_scratch(z)], flops=matmul_flops(z, 1),
    )


def saved_spec(z):
    return pl.BlockSpec((1, z.rows, z.block), lambda i, s: (s[2], 0, 0))


def backward_in(z, scalars, k, top, incoming, weight, gy_saved):
    has_top = k < z.micro

    def body(s, *refs):
        if has_top:
            t, inc, w, _, *rest = refs
        else:
            inc, w, _, *rest = refs
        gy, rest = rest[0], rest[1:]
        if has_top:
            plain, rest = rest[0], rest[1:]
        pieces, wire = rest[: z.hidden], rest[z.hidden]

        if has_top:

            @pl.when(s[1] == 0)
            def _():
                unit = unit_matrix(z)

                def one(pair):
                    parts = []
                    for g in range(z.groups):
                        start = pl.multiple_of((g * z.pairs + pair) * z.block, z.block)
                        parts.append(t[:, pl.ds(start, z.block)])
                    values = jnp.concatenate(parts, axis=0)
                    plain[pair_rows(z, pair), :] = dot(unit, values, NT).astype(jnp.bfloat16)

                loop(z.pairs, one)

            @pl.when(s[1] != 0)
            def _():
                plain[...] = inc[...]

            held = plain
        else:
            held = inc

        def one(pair):
            at = pair_rows(z, pair)
            value = held[at, :]
            gy[0, at, :] = value
            for g, repeated in enumerate(spread(z, value.astype(jnp.float32))):
                index = g * z.pairs + pair
                produce(z, wire, block_rows(z, w, index), repeated, index)

        loop(z.pairs, one)
        send_pieces(z, wire, s[0], pieces)

    flat = (z.rows, z.block)
    args = [incoming, weight, gy_saved]
    specs = [whole(flat), whole(weight.shape), ANY]
    if has_top:
        args = [top] + args
        specs = [pl.BlockSpec((z.tokens, z.width), lambda i, s: (k, 0))] + specs
    outs = [jax.ShapeDtypeStruct(gy_saved.shape, gy_saved.dtype)]
    out_specs = [saved_spec(z)]
    if has_top:
        outs.append(bf16(*flat))
        out_specs.append(whole(flat))
    got = call(
        body, "backward_in", scalars, args, specs,
        outs + piece_shapes(z), out_specs + piece_specs(z), [wire_scratch(z)],
        aliases={len(args): 0}, flops=matmul_flops(z, 1),
    )
    if has_top:
        return got[0], got[1], got[2:]
    return got[0], incoming, got[1:]


def backward_wide(z, scalars, pieces, weight_rs, weight_lf, options, gw_saved, gp_saved):
    def body(s, *refs):
        ins, refs = refs[: z.hidden], refs[z.hidden :]
        rs, lf, refs = refs[0], refs[1], refs[2:]
        derivs, refs = refs[: len(options)], refs[len(options) + 2 :]
        gw, gp, refs = refs[0], refs[1], refs[2:]
        out, (wire, deriv, sem) = refs[: z.hidden], refs[z.hidden :]
        if len(options) == 1:
            pltpu.make_async_copy(derivs[0], deriv, sem).start()
        else:
            first, last = options[0][0], options[-1][0]
            for (where, _), ref in zip(options, derivs):
                here = s[1] == where
                if where == first:
                    here = s[1] <= where
                elif where == last:
                    here = s[1] >= where

                @pl.when(here)
                def _():
                    pltpu.make_async_copy(ref, deriv, sem).start()

        loop(z.pairs, lambda pair: place(z, ins, s[0], pair, gw.at[0]))
        pltpu.make_async_copy(derivs[0], deriv, sem).wait()

        def one(pair):
            at = pair_rows(z, pair)
            grad = consume(z, rs, gw[0, at, :], pair) * deriv[at, :].astype(jnp.float32)
            rounded = grad.astype(jnp.bfloat16)
            gp[0, at, :] = rounded
            for g, repeated in enumerate(spread(z, rounded.astype(jnp.float32))):
                index = g * z.pairs + pair
                produce(z, wire, block_rows(z, lf, index), repeated, index)

        loop(z.pairs, one)
        send_pieces(z, wire, s[0], out)

    args = [*pieces, weight_rs, weight_lf, *[d for _, d in options], gw_saved, gp_saved]
    first = len(args) - 1
    got = call(
        body, "backward_wide", scalars, args,
        piece_specs(z) + [whole(weight_rs.shape)] * 2 + [ANY] * (len(options) + 2),
        [jax.ShapeDtypeStruct(a.shape, a.dtype) for a in (gw_saved, gp_saved)] + piece_shapes(z),
        [saved_spec(z)] * 2 + piece_specs(z),
        [wire_scratch(z), pltpu.VMEM((z.rows, z.block), jnp.bfloat16), pltpu.SemaphoreType.DMA],
        aliases={first: 0, first + 1: 1}, flops=matmul_flops(z, 2),
    )
    return got[0], got[1], got[2:]


def backward_out(z, scalars, pieces, weight, gy, gn_saved, adj_saved):
    def body(s, *refs):
        ins, (w, g_ref, _, _, gn, adj, nxt) = refs[: z.hidden], refs[z.hidden :]

        def one(pair):
            at = pair_rows(z, pair)
            place(z, ins, s[0], pair, gn.at[0])
            grad = consume(z, w, gn[0, at, :], pair)
            value = (g_ref[at, :].astype(jnp.float32) + grad).astype(jnp.bfloat16)
            adj[0, at, :] = value
            nxt[at, :] = value

        loop(z.pairs, one)

    args = [*pieces, weight, gy, gn_saved, adj_saved]
    flat = (z.rows, z.block)
    return call(
        body, "backward_out", scalars, args,
        piece_specs(z) + [whole(weight.shape), whole(flat), ANY, ANY],
        [jax.ShapeDtypeStruct(a.shape, a.dtype) for a in (gn_saved, adj_saved)] + [bf16(*flat)],
        [saved_spec(z)] * 2 + [whole(flat)],
        aliases={len(args) - 1: 0, len(args): 1}, flops=matmul_flops(z, 1),
    )


def all_saved(z):
    return pl.BlockSpec((z.micro, z.rows, z.block), lambda i, s: (0, 0, 0))


def gradient(z, scalars, name, left, right, kind, shared):
    right_args = {"saved": [right], "rows": [right]}.get(kind)
    if kind == "list":
        right_args = list(right)
    elif kind == "pieces":
        right_args = [p for group in right for p in group]
    count = z.share * z.block

    def body(s, l, *refs):
        ins, refs = refs[: len(right_args)], refs[len(right_args) :]
        outs = refs[: z.tok]
        if kind == "pieces":
            held = refs[z.tok]
            for m in range(z.micro):
                group = ins[m * z.hidden : (m + 1) * z.hidden]
                loop(z.pairs, lambda pair: place(z, group, s[0], pair, held.at[m]))

        group_of = lane_group(z, z.block)
        for d, out in enumerate(outs):
            owner = partner(s[3], d, z.tok) * z.share

            def one(i):
                index = owner + i
                g = lax.div(index, z.pairs)
                pair = index - g * z.pairs
                at = pair_rows(z, pair)
                total = None
                for m in range(z.micro):
                    a = l[m, at, :]
                    a = jnp.where(group_of == g, a, jnp.zeros_like(a))
                    if kind == "rows":
                        rows = []
                        for q in range(z.groups):
                            start = pl.multiple_of((q * z.pairs + pair) * z.block, z.block)
                            rows.append(
                                ins[0][m * z.tokens : (m + 1) * z.tokens, pl.ds(start, z.block)]
                            )
                        term = dot(a, jnp.concatenate(rows, axis=0))
                    else:
                        if kind == "saved":
                            b = ins[0][m, at, :]
                        elif kind == "list":
                            b = ins[m][at, :]
                        else:
                            b = held[m, at, :]
                        term = dot(a, b, NT)
                    total = term if total is None else total + term
                out[pair_rows(z, i), :] = total.astype(out.dtype)

            loop(z.share, one)

    if kind == "saved":
        specs = [all_saved(z)]
    else:
        specs = [whole(a.shape) for a in right_args]
    scratch = []
    if kind == "pieces":
        scratch = [pltpu.VMEM((z.micro, z.rows, z.block), jnp.bfloat16)]
    got = call(
        body, name, scalars, [left, *right_args], [all_saved(z)] + specs,
        [f32(count, z.block)] + [bf16(count, z.block)] * (z.tok - 1),
        [whole((count, z.block))] * z.tok, scratch, flops=matmul_flops(z, z.micro),
    )
    received = exchange(got, "tok")
    total = received[0]
    for other in received[1:]:
        total = total + other.astype(jnp.float32)
    return (total * shared).reshape(1, z.share, z.block, z.block)


def token_rows(z, scalars, saved):
    def body(s, a, out):
        for m in range(z.micro):

            def one(pair):
                turned = a[m, pair_rows(z, pair), :].astype(jnp.float32).T.astype(jnp.bfloat16)
                for g in range(z.groups):
                    start = pl.multiple_of((g * z.pairs + pair) * z.block, z.block)
                    out[m * z.tokens : (m + 1) * z.tokens, pl.ds(start, z.block)] = turned[
                        g * z.tokens : (g + 1) * z.tokens
                    ]

            loop(z.pairs, one)

    return call(
        body, "token_rows", scalars, [saved], [all_saved(z)],
        [bf16(z.tok_rows, z.width)], [whole((z.tok_rows, z.width))],
    )[0]


def on_device(section_inputs, top_adjoint, right_first, left_first, right_second, left_second):
    sections = lax.axis_size("section")
    token_count = lax.axis_size("tok")
    hidden_count = lax.axis_size("hidden")
    _, share, block, _ = right_first.shape
    inputs = section_inputs[0]
    tok_rows = inputs.shape[0]
    z = Shape(hidden_count, token_count, share * token_count, block, tok_rows)
    hid = lax.axis_index("hidden")
    depth = sections - 1 - lax.axis_index("section")
    tok = lax.axis_index("tok")
    shared = 1.0 / math.sqrt(tok_rows * token_count)

    def scalars_of(slot):
        return jnp.stack([hid, depth, slot, tok]).astype(jnp.int32)

    base = scalars_of(jnp.int32(0))

    def gathered(weight, forms):
        own = weight.reshape(share * block, block)
        return prepare(z, base, exchange([own] * token_count, "tok"), forms)

    rf_mid, rf_out = gathered(right_first, ("p", "t"))
    (ls_in,) = gathered(left_second, ("tp",))
    lf_mid, lf_back = gathered(left_first, ("n", "tp"))
    rs_back, rs_mid = gathered(right_second, ("t", "p"))

    saved = jnp.zeros((z.micro + 1, z.rows, z.block), jnp.bfloat16)
    gy_saved = gw_saved = gp_saved = gn_saved = adj_saved = saved
    zero = jnp.zeros((z.rows, z.block), jnp.bfloat16)
    ticks = z.micro + SKEW * (sections - 1)
    arrivals = {}
    wides, acts, derivs, seconds = [], [], [], []

    for k in range(ticks):
        micro = k - SKEW * depth
        active = jnp.logical_and(micro >= 0, micro < z.micro)
        scalars = scalars_of(jnp.where(active, micro, z.micro))
        if k < z.micro:
            mid = first_mid(z, base, k, inputs, rf_mid)
            wide, act, deriv = forward_wide(z, base, exchange(mid, "hidden"), lf_mid)
            wides.append(wide)
            acts.append(act)
            derivs.append(deriv)
        incoming = arrivals.get(k, zero)
        gy_saved, gy, pieces = backward_in(
            z, scalars, k, top_adjoint, incoming, ls_in, gy_saved
        )
        options = [
            (c, derivs[k - SKEW * c])
            for c in range(sections)
            if 0 <= k - SKEW * c < z.micro
        ]
        gw_saved, gp_saved, pieces = backward_wide(
            z, scalars, exchange(pieces, "hidden"), rs_back, lf_back, options, gw_saved, gp_saved
        )
        gn_saved, adj_saved, nxt = backward_out(
            z, scalars, exchange(pieces, "hidden"), rf_out, gy, gn_saved, adj_saved
        )
        if k + SKEW < ticks:
            route = [(i, i - 1) for i in range(1, sections)]
            arrivals[k + SKEW] = lax.ppermute(nxt, "section", route)
        if k < z.micro:
            seconds.append(exchange(second_mid(z, base, acts[k], rs_mid), "hidden"))

    grad_ls = gradient(z, base, "grad_ls", gy_saved, seconds, "pieces", shared)
    grad_rs = gradient(z, base, "grad_rs", gw_saved, acts, "list", shared)
    grad_lf = gradient(z, base, "grad_lf", gp_saved, wides, "list", shared)
    grad_rf = gradient(z, base, "grad_rf", gn_saved, inputs, "rows", shared)
    adjoints = token_rows(z, base, adj_saved)
    return adjoints[None], grad_rf, grad_lf, grad_rs, grad_ls


def solution(mesh):
    blocks = P("section", ("hidden", "tok"), None, None)
    rows = P("section", "tok", "hidden")
    return jax.shard_map(
        on_device,
        mesh=mesh,
        in_specs=(rows, P("tok", "hidden"), blocks, blocks, blocks, blocks),
        out_specs=(rows, blocks, blocks, blocks, blocks),
        check_vma=False,
    )
```

```python
import functools
import math

import jax
import jax.numpy as jnp
from jax import lax
from jax.experimental import pallas as pl
from jax.experimental.pallas import tpu as pltpu
from jax.sharding import PartitionSpec as P

GROUPS = 2
SKEW = 2
UNROLL = 4


gelu_coef = 0.7978845608028654
NT = (((1,), (1,)), ((), ()))
NN = (((1,), (0,)), ((), ()))


def gelu_parts(preact):
    inner_arg = gelu_coef * (preact + 0.044715 * preact * preact * preact)
    squashed = jnp.tanh(inner_arg)
    activation = 0.5 * preact * (1.0 + squashed)
    derivative = 0.5 * (1.0 + squashed) + 0.5 * preact * (1.0 - squashed * squashed) * gelu_coef * (
        1.0 + 3.0 * 0.044715 * preact * preact
    )
    return (activation, derivative)


def dot(a, b, dims=NN):
    return lax.dot_general(a, b, dims, preferred_element_type=jnp.float32)


def partner(me, distance, count):
    if count & (count - 1) == 0:
        return me ^ distance
    return lax.rem(me + distance, count)


def source(me, distance, count):
    if count & (count - 1) == 0:
        return me ^ distance
    return lax.rem(me + count - distance, count)


def exchange(pieces, axis):
    count = len(pieces)
    out = [pieces[0]]
    for distance in range(1, count):
        if count & (count - 1) == 0:
            route = [(i, i ^ distance) for i in range(count)]
        else:
            route = [(i, (i + distance) % count) for i in range(count)]
        out.append(lax.ppermute(pieces[distance], axis, route))
    return out


class Shape:
    def __init__(self, hidden_count, token_count, local_count, block, tok_rows):
        self.hidden = hidden_count
        self.tok = token_count
        self.local = local_count
        self.block = block
        self.groups = GROUPS
        self.pairs = local_count // GROUPS
        self.tokens = block // GROUPS
        self.micro = tok_rows // self.tokens
        self.share = local_count // token_count
        self.rows = self.pairs * block
        self.picked = block // GROUPS
        self.piece = self.pairs * local_count
        self.pitch = local_count + 8
        self.tok_rows = tok_rows
        self.width = local_count * block


def lane_group(z, rows):
    return lax.broadcasted_iota(jnp.int32, (rows, z.block), 1) // z.tokens


def pick(parts, group):
    out = parts[0]
    for g in range(1, len(parts)):
        out = jnp.where(group == g, parts[g], out)
    return out


def spread(z, values):
    turned = [values] + [
        pltpu.roll(values, s * z.tokens, 1) for s in range(1, z.groups)
    ]
    group = lane_group(z, values.shape[0])
    return [
        pick([turned[(q - g) % z.groups] for q in range(z.groups)], group).astype(jnp.bfloat16)
        for g in range(z.groups)
    ]


def produce(z, wire, weight, values, index):
    full = dot(weight, values)
    parts = [full[g * z.picked : (g + 1) * z.picked] for g in range(z.groups)]
    wire[pl.ds(index, z.picked, stride=z.pitch), :] = pick(parts, lane_group(z, z.picked))


def send_pieces(z, wire, hid, piece_refs):
    for d, ref in enumerate(piece_refs):
        first = partner(hid, d, z.hidden) * z.pairs
        for pair in range(z.pairs):
            start = pl.multiple_of((first + pair) * z.pitch, 8)
            ref[pair * z.local : (pair + 1) * z.local, :] = wire[
                pl.ds(start, z.local), :
            ].astype(jnp.bfloat16)


def block_rows(z, ref, index):
    return ref[pl.ds(pl.multiple_of(index * z.block, z.block), z.block), :]


def pair_rows(z, pair):
    return pl.ds(pl.multiple_of(pair * z.block, z.block), z.block)


def place(z, piece_refs, hid, pair, ref):
    for d, piece in enumerate(piece_refs):
        src = source(hid, d, z.hidden)
        start = pl.multiple_of(pair * z.block + src * z.local, z.local)
        ref[pl.ds(start, z.local), :] = piece[
            pl.ds(pl.multiple_of(pair * z.local, z.local), z.local), :
        ]


def consume(z, weight_ref, values, pair):
    parts = [dot(block_rows(z, weight_ref, g * z.pairs + pair), values) for g in range(z.groups)]
    return pick(parts, lane_group(z, z.block))


def loop(count, body, unroll=UNROLL):
    def step(i, carry):
        body(i)
        return carry

    lax.fori_loop(0, count, step, 0, unroll=unroll)


def whole(shape):
    return pl.BlockSpec(shape, lambda i, s: tuple(0 for _ in shape))


ANY = pl.BlockSpec(memory_space=pl.ANY)


def call(body, name, scalars, args, in_specs, outs, out_specs, scratch=(), aliases=None, flops=0, grant=12):
    size = lambda a: math.prod(a.shape) * a.dtype.itemsize
    moved = sum(size(a) for a, s in zip(args, in_specs) if s.block_shape is not None)
    moved += sum(size(o) for o in outs if o.shape[0] < 10**9)
    return pl.pallas_call(
        body,
        name=name,
        grid_spec=pltpu.PrefetchScalarGridSpec(
            num_scalar_prefetch=1,
            grid=(1,),
            in_specs=in_specs,
            out_specs=out_specs,
            scratch_shapes=list(scratch),
        ),
        out_shape=outs,
        input_output_aliases=aliases or {},
        cost_estimate=pl.CostEstimate(flops=flops, bytes_accessed=moved, transcendentals=0),
        compiler_params=pltpu.CompilerParams(vmem_limit_bytes=grant * 2**20),
    )(scalars, *args)


def bf16(*shape):
    return jax.ShapeDtypeStruct(shape, jnp.bfloat16)


def f32(*shape):
    return jax.ShapeDtypeStruct(shape, jnp.float32)


def shuffle_matrix(z):
    row = lax.broadcasted_iota(jnp.int32, (z.block, z.block), 0)
    col = lax.broadcasted_iota(jnp.int32, (z.block, z.block), 1)
    g = row // z.picked
    rest = row - g * z.picked
    h = rest // z.pairs
    pair = rest - h * z.pairs
    return (col == h * z.local + g * z.pairs + pair).astype(jnp.bfloat16)


def unit_matrix(z):
    row = lax.broadcasted_iota(jnp.int32, (z.block, z.block), 0)
    col = lax.broadcasted_iota(jnp.int32, (z.block, z.block), 1)
    return (col == row).astype(jnp.bfloat16)


def prepare(z, scalars, pieces, forms):
    def body(s, *refs):
        ins, outs = refs[: z.tok], refs[z.tok :]
        unit, shuffle = unit_matrix(z), shuffle_matrix(z)
        for d, piece in enumerate(ins):
            first = source(s[3], d, z.tok) * z.share

            def one(i):
                w = block_rows(z, piece, i)
                at = pair_rows(z, first + i)
                for form, out in zip(forms, outs):
                    if form == "n":
                        out[at, :] = w
                    else:
                        left = shuffle if "p" in form else unit
                        out[at, :] = dot(left, w, NT if "t" in form else NN).astype(jnp.bfloat16)

            loop(z.share, one)

    size = z.local * z.block
    return call(
        body, "prepare", scalars, pieces,
        [whole((z.share * z.block, z.block))] * z.tok,
        [bf16(size, z.block)] * len(forms), [whole((size, z.block))] * len(forms),
    )


def piece_specs(z):
    return [whole((z.piece, z.block))] * z.hidden


def piece_shapes(z):
    return [bf16(z.piece, z.block)] * z.hidden


def wire_scratch(z):
    return pltpu.VMEM((z.picked * z.pitch, z.block), jnp.float32)


def matmul_flops(z, count):
    return 2 * count * z.local * z.block**3


def first_mid(z, scalars, m, inputs, weight):
    def body(s, x, w, *rest):
        pieces, wire = rest[: z.hidden], rest[z.hidden]

        def one(b):
            cols = pl.ds(pl.multiple_of(b * z.block, z.block), z.block)
            xb = x[:, cols]
            values = jnp.concatenate([xb] * z.groups, axis=0)
            full = dot(block_rows(z, w, b), values, NT)
            parts = [full[g * z.picked : (g + 1) * z.picked] for g in range(z.groups)]
            wire[pl.ds(b, z.picked, stride=z.pitch), :] = pick(parts, lane_group(z, z.picked))

        loop(z.local, one)
        send_pieces(z, wire, s[0], pieces)

    return call(
        body, "first_mid", scalars, [inputs, weight],
        [pl.BlockSpec((z.tokens, z.width), lambda i, s: (m, 0)), whole(weight.shape)],
        piece_shapes(z), piece_specs(z), [wire_scratch(z)], flops=matmul_flops(z, 1),
    )


def forward_wide(z, scalars, pieces, weight):
    def body(s, *refs):
        ins, w = refs[: z.hidden], refs[z.hidden]
        fw, act, deriv = refs[z.hidden + 1 :]

        def one(pair):
            place(z, ins, s[0], pair, fw)
            at = pair_rows(z, pair)
            a, d = gelu_parts(consume(z, w, fw[at, :], pair))
            act[at, :] = a.astype(jnp.bfloat16)
            deriv[at, :] = d.astype(jnp.bfloat16)

        loop(z.pairs, one)

    return call(
        body, "forward_wide", scalars, [*pieces, weight],
        piece_specs(z) + [whole(weight.shape)],
        [bf16(z.rows, z.block)] * 3, [whole((z.rows, z.block))] * 3, flops=matmul_flops(z, 1),
    )


def second_mid(z, scalars, act, weight):
    def body(s, a, w, *rest):
        pieces, wire = rest[: z.hidden], rest[z.hidden]

        def one(pair):
            values = a[pair_rows(z, pair), :].astype(jnp.float32)
            for g, repeated in enumerate(spread(z, values)):
                index = g * z.pairs + pair
                produce(z, wire, block_rows(z, w, index), repeated, index)

        loop(z.pairs, one)
        send_pieces(z, wire, s[0], pieces)

    return call(
        body, "second_mid", scalars, [act, weight],
        [whole(act.shape), whole(weight.shape)],
        piece_shapes(z), piece_specs(z), [wire_scratch(z)], flops=matmul_flops(z, 1),
    )


def saved_spec(z):
    return pl.BlockSpec((1, z.rows, z.block), lambda i, s: (s[2], 0, 0))


def backward_in(z, scalars, k, top, incoming, weight, gy_saved):
    has_top = k < z.micro

    def body(s, *refs):
        if has_top:
            t, inc, w, _, *rest = refs
        else:
            inc, w, _, *rest = refs
        gy, rest = rest[0], rest[1:]
        if has_top:
            plain, rest = rest[0], rest[1:]
        pieces, wire = rest[: z.hidden], rest[z.hidden]

        if has_top:

            @pl.when(s[1] == 0)
            def _():
                unit = unit_matrix(z)

                def one(pair):
                    parts = []
                    for g in range(z.groups):
                        start = pl.multiple_of((g * z.pairs + pair) * z.block, z.block)
                        parts.append(t[:, pl.ds(start, z.block)])
                    values = jnp.concatenate(parts, axis=0)
                    plain[pair_rows(z, pair), :] = dot(unit, values, NT).astype(jnp.bfloat16)

                loop(z.pairs, one)

            @pl.when(s[1] != 0)
            def _():
                plain[...] = inc[...]

            held = plain
        else:
            held = inc

        def one(pair):
            at = pair_rows(z, pair)
            value = held[at, :]
            gy[0, at, :] = value
            for g, repeated in enumerate(spread(z, value.astype(jnp.float32))):
                index = g * z.pairs + pair
                produce(z, wire, block_rows(z, w, index), repeated, index)

        loop(z.pairs, one)
        send_pieces(z, wire, s[0], pieces)

    flat = (z.rows, z.block)
    args = [incoming, weight, gy_saved]
    specs = [whole(flat), whole(weight.shape), ANY]
    if has_top:
        args = [top] + args
        specs = [pl.BlockSpec((z.tokens, z.width), lambda i, s: (k, 0))] + specs
    outs = [jax.ShapeDtypeStruct(gy_saved.shape, gy_saved.dtype)]
    out_specs = [saved_spec(z)]
    if has_top:
        outs.append(bf16(*flat))
        out_specs.append(whole(flat))
    got = call(
        body, "backward_in", scalars, args, specs,
        outs + piece_shapes(z), out_specs + piece_specs(z), [wire_scratch(z)],
        aliases={len(args): 0}, flops=matmul_flops(z, 1),
    )
    if has_top:
        return got[0], got[1], got[2:]
    return got[0], incoming, got[1:]


def backward_wide(z, scalars, pieces, weight_rs, weight_lf, options, gw_saved, gp_saved):
    def body(s, *refs):
        ins, refs = refs[: z.hidden], refs[z.hidden :]
        rs, lf, refs = refs[0], refs[1], refs[2:]
        derivs, refs = refs[: len(options)], refs[len(options) + 2 :]
        gw, gp, refs = refs[0], refs[1], refs[2:]
        out, (wire, deriv, sem) = refs[: z.hidden], refs[z.hidden :]
        if len(options) == 1:
            pltpu.make_async_copy(derivs[0], deriv, sem).start()
        else:
            first, last = options[0][0], options[-1][0]
            for (where, _), ref in zip(options, derivs):
                here = s[1] == where
                if where == first:
                    here = s[1] <= where
                elif where == last:
                    here = s[1] >= where

                @pl.when(here)
                def _():
                    pltpu.make_async_copy(ref, deriv, sem).start()

        loop(z.pairs, lambda pair: place(z, ins, s[0], pair, gw.at[0]))
        pltpu.make_async_copy(derivs[0], deriv, sem).wait()

        def one(pair):
            at = pair_rows(z, pair)
            grad = consume(z, rs, gw[0, at, :], pair) * deriv[at, :].astype(jnp.float32)
            rounded = grad.astype(jnp.bfloat16)
            gp[0, at, :] = rounded
            for g, repeated in enumerate(spread(z, rounded.astype(jnp.float32))):
                index = g * z.pairs + pair
                produce(z, wire, block_rows(z, lf, index), repeated, index)

        loop(z.pairs, one)
        send_pieces(z, wire, s[0], out)

    args = [*pieces, weight_rs, weight_lf, *[d for _, d in options], gw_saved, gp_saved]
    first = len(args) - 1
    got = call(
        body, "backward_wide", scalars, args,
        piece_specs(z) + [whole(weight_rs.shape)] * 2 + [ANY] * (len(options) + 2),
        [jax.ShapeDtypeStruct(a.shape, a.dtype) for a in (gw_saved, gp_saved)] + piece_shapes(z),
        [saved_spec(z)] * 2 + piece_specs(z),
        [wire_scratch(z), pltpu.VMEM((z.rows, z.block), jnp.bfloat16), pltpu.SemaphoreType.DMA],
        aliases={first: 0, first + 1: 1}, flops=matmul_flops(z, 2),
    )
    return got[0], got[1], got[2:]


def backward_out(z, scalars, pieces, weight, gy, gn_saved, adj_saved):
    def body(s, *refs):
        ins, (w, g_ref, _, _, gn, adj, nxt) = refs[: z.hidden], refs[z.hidden :]

        def one(pair):
            at = pair_rows(z, pair)
            place(z, ins, s[0], pair, gn.at[0])
            grad = consume(z, w, gn[0, at, :], pair)
            value = (g_ref[at, :].astype(jnp.float32) + grad).astype(jnp.bfloat16)
            adj[0, at, :] = value
            nxt[at, :] = value

        loop(z.pairs, one)

    args = [*pieces, weight, gy, gn_saved, adj_saved]
    flat = (z.rows, z.block)
    return call(
        body, "backward_out", scalars, args,
        piece_specs(z) + [whole(weight.shape), whole(flat), ANY, ANY],
        [jax.ShapeDtypeStruct(a.shape, a.dtype) for a in (gn_saved, adj_saved)] + [bf16(*flat)],
        [saved_spec(z)] * 2 + [whole(flat)],
        aliases={len(args) - 1: 0, len(args): 1}, flops=matmul_flops(z, 1),
    )


def all_saved(z):
    return pl.BlockSpec((z.micro, z.rows, z.block), lambda i, s: (0, 0, 0))


def gradient(z, scalars, name, left, right, kind, shared):
    right_args = {"saved": [right], "rows": [right]}.get(kind)
    if kind == "list":
        right_args = list(right)
    elif kind == "pieces":
        right_args = [p for group in right for p in group]
    count = z.share * z.block

    def body(s, l, *refs):
        ins, refs = refs[: len(right_args)], refs[len(right_args) :]
        outs = refs[: z.tok]
        if kind == "pieces":
            held = refs[z.tok]
            for m in range(z.micro):
                group = ins[m * z.hidden : (m + 1) * z.hidden]
                loop(z.pairs, lambda pair: place(z, group, s[0], pair, held.at[m]))

        group_of = lane_group(z, z.block)
        for d, out in enumerate(outs):
            owner = partner(s[3], d, z.tok) * z.share

            def one(i):
                index = owner + i
                g = lax.div(index, z.pairs)
                pair = index - g * z.pairs
                at = pair_rows(z, pair)
                total = None
                for m in range(z.micro):
                    a = l[m, at, :]
                    a = jnp.where(group_of == g, a, jnp.zeros_like(a))
                    if kind == "rows":
                        rows = []
                        for q in range(z.groups):
                            start = pl.multiple_of((q * z.pairs + pair) * z.block, z.block)
                            rows.append(
                                ins[0][m * z.tokens : (m + 1) * z.tokens, pl.ds(start, z.block)]
                            )
                        term = dot(a, jnp.concatenate(rows, axis=0))
                    else:
                        if kind == "saved":
                            b = ins[0][m, at, :]
                        elif kind == "list":
                            b = ins[m][at, :]
                        else:
                            b = held[m, at, :]
                        term = dot(a, b, NT)
                    total = term if total is None else total + term
                out[pair_rows(z, i), :] = total.astype(out.dtype)

            loop(z.share, one)

    if kind == "saved":
        specs = [all_saved(z)]
    else:
        specs = [whole(a.shape) for a in right_args]
    scratch = []
    if kind == "pieces":
        scratch = [pltpu.VMEM((z.micro, z.rows, z.block), jnp.bfloat16)]
    got = call(
        body, name, scalars, [left, *right_args], [all_saved(z)] + specs,
        [f32(count, z.block)] + [bf16(count, z.block)] * (z.tok - 1),
        [whole((count, z.block))] * z.tok, scratch, flops=matmul_flops(z, z.micro), grant=28,
    )
    received = exchange(got, "tok")
    total = received[0]
    for other in received[1:]:
        total = total + other.astype(jnp.float32)
    return (total * shared).reshape(1, z.share, z.block, z.block)


def token_rows(z, scalars, saved):
    def body(s, a, out):
        for m in range(z.micro):

            def one(pair):
                turned = a[m, pair_rows(z, pair), :].astype(jnp.float32).T.astype(jnp.bfloat16)
                for g in range(z.groups):
                    start = pl.multiple_of((g * z.pairs + pair) * z.block, z.block)
                    out[m * z.tokens : (m + 1) * z.tokens, pl.ds(start, z.block)] = turned[
                        g * z.tokens : (g + 1) * z.tokens
                    ]

            loop(z.pairs, one)

    return call(
        body, "token_rows", scalars, [saved], [all_saved(z)],
        [bf16(z.tok_rows, z.width)], [whole((z.tok_rows, z.width))], grant=28,
    )[0]


def on_device(section_inputs, top_adjoint, right_first, left_first, right_second, left_second):
    sections = lax.axis_size("section")
    token_count = lax.axis_size("tok")
    hidden_count = lax.axis_size("hidden")
    _, share, block, _ = right_first.shape
    inputs = section_inputs[0]
    tok_rows = inputs.shape[0]
    z = Shape(hidden_count, token_count, share * token_count, block, tok_rows)
    hid = lax.axis_index("hidden")
    depth = sections - 1 - lax.axis_index("section")
    tok = lax.axis_index("tok")
    shared = 1.0 / math.sqrt(tok_rows * token_count)

    def scalars_of(slot):
        return jnp.stack([hid, depth, slot, tok]).astype(jnp.int32)

    base = scalars_of(jnp.int32(0))

    def gathered(weight, forms):
        own = weight.reshape(share * block, block)
        return prepare(z, base, exchange([own] * token_count, "tok"), forms)

    rf_mid, rf_out = gathered(right_first, ("p", "t"))
    (ls_in,) = gathered(left_second, ("tp",))
    lf_mid, lf_back = gathered(left_first, ("n", "tp"))
    rs_back, rs_mid = gathered(right_second, ("t", "p"))

    saved = jnp.zeros((z.micro + 1, z.rows, z.block), jnp.bfloat16)
    gy_saved = gw_saved = gp_saved = gn_saved = adj_saved = saved
    zero = jnp.zeros((z.rows, z.block), jnp.bfloat16)
    ticks = z.micro + SKEW * (sections - 1)
    arrivals = {}
    wides, acts, derivs, seconds = [], [], [], []

    for k in range(ticks):
        micro = k - SKEW * depth
        active = jnp.logical_and(micro >= 0, micro < z.micro)
        scalars = scalars_of(jnp.where(active, micro, z.micro))
        if k < z.micro:
            mid = first_mid(z, base, k, inputs, rf_mid)
            wide, act, deriv = forward_wide(z, base, exchange(mid, "hidden"), lf_mid)
            wides.append(wide)
            acts.append(act)
            derivs.append(deriv)
        incoming = arrivals.get(k, zero)
        gy_saved, gy, pieces = backward_in(
            z, scalars, k, top_adjoint, incoming, ls_in, gy_saved
        )
        options = [
            (c, derivs[k - SKEW * c])
            for c in range(sections)
            if 0 <= k - SKEW * c < z.micro
        ]
        gw_saved, gp_saved, pieces = backward_wide(
            z, scalars, exchange(pieces, "hidden"), rs_back, lf_back, options, gw_saved, gp_saved
        )
        gn_saved, adj_saved, nxt = backward_out(
            z, scalars, exchange(pieces, "hidden"), rf_out, gy, gn_saved, adj_saved
        )
        if k + SKEW < ticks:
            route = [(i, i - 1) for i in range(1, sections)]
            arrivals[k + SKEW] = lax.ppermute(nxt, "section", route)
        if k < z.micro:
            seconds.append(exchange(second_mid(z, base, acts[k], rs_mid), "hidden"))

    grad_ls = gradient(z, base, "grad_ls", gy_saved, seconds, "pieces", shared)
    grad_rs = gradient(z, base, "grad_rs", gw_saved, acts, "list", shared)
    grad_lf = gradient(z, base, "grad_lf", gp_saved, wides, "list", shared)
    grad_rf = gradient(z, base, "grad_rf", gn_saved, inputs, "rows", shared)
    adjoints = token_rows(z, base, adj_saved)
    return adjoints[None], grad_rf, grad_lf, grad_rs, grad_ls


def solution(mesh):
    blocks = P("section", ("hidden", "tok"), None, None)
    rows = P("section", "tok", "hidden")
    return jax.shard_map(
        on_device,
        mesh=mesh,
        in_specs=(rows, P("tok", "hidden"), blocks, blocks, blocks, blocks),
        out_specs=(rows, blocks, blocks, blocks, blocks),
        check_vma=False,
    )
```

```python
import math

import jax
import jax.numpy as jnp
from jax import lax
from jax.experimental import pallas as pl
from jax.experimental.pallas import tpu as pltpu
from jax.sharding import PartitionSpec as P


GROUPS = 2
SKEW = 2
UNROLL = 4


gelu_coef = 0.7978845608028654
NT = (((1,), (1,)), ((), ()))
NN = (((1,), (0,)), ((), ()))


def gelu_parts(preact):
    inner_arg = gelu_coef * (preact + 0.044715 * preact * preact * preact)
    squashed = jnp.tanh(inner_arg)
    activation = 0.5 * preact * (1.0 + squashed)
    derivative = 0.5 * (1.0 + squashed) + 0.5 * preact * (1.0 - squashed * squashed) * gelu_coef * (
        1.0 + 3.0 * 0.044715 * preact * preact
    )
    return (activation, derivative)


def dot(a, b, dims=NN):
    return lax.dot_general(a, b, dims, preferred_element_type=jnp.float32)


def partner(me, distance, count):
    if count & (count - 1) == 0:
        return me ^ distance
    return lax.rem(me + distance, count)


def source(me, distance, count):
    if count & (count - 1) == 0:
        return me ^ distance
    return lax.rem(me + count - distance, count)


def exchange(pieces, axis):
    count = len(pieces)
    out = [pieces[0]]
    for distance in range(1, count):
        if count & (count - 1) == 0:
            route = [(i, i ^ distance) for i in range(count)]
        else:
            route = [(i, (i + distance) % count) for i in range(count)]
        out.append(lax.ppermute(pieces[distance], axis, route))
    return out


class Shape:
    def __init__(self, hidden_count, token_count, local_count, block, tok_rows):
        self.hidden = hidden_count
        self.tok = token_count
        self.local = local_count
        self.block = block
        self.groups = GROUPS
        self.pairs = local_count // GROUPS
        self.tokens = block // GROUPS
        self.micro = tok_rows // self.tokens
        self.share = local_count // token_count
        self.rows = self.pairs * block
        self.picked = block // GROUPS
        self.piece = self.pairs * local_count
        self.pitch = local_count + 8
        self.tok_rows = tok_rows
        self.width = local_count * block


def lane_group(z, rows):
    return lax.broadcasted_iota(jnp.int32, (rows, z.block), 1) // z.tokens


def pick(parts, group):
    out = parts[0]
    for g in range(1, len(parts)):
        out = jnp.where(group == g, parts[g], out)
    return out


def spread(z, values):
    turned = [values] + [
        pltpu.roll(values, s * z.tokens, 1) for s in range(1, z.groups)
    ]
    group = lane_group(z, values.shape[0])
    return [
        pick([turned[(q - g) % z.groups] for q in range(z.groups)], group).astype(jnp.bfloat16)
        for g in range(z.groups)
    ]


def produce(z, wire, weight, values, index):
    full = dot(weight, values)
    parts = [full[g * z.picked : (g + 1) * z.picked] for g in range(z.groups)]
    wire[pl.ds(index, z.picked, stride=z.pitch), :] = pick(parts, lane_group(z, z.picked))


def send_pieces(z, wire, hid, piece_refs):
    for d, ref in enumerate(piece_refs):
        first = partner(hid, d, z.hidden) * z.pairs

        def one(pair):
            start = pl.multiple_of((first + pair) * z.pitch, 8)
            at = pl.multiple_of(pair * z.local, z.local)
            ref[pl.ds(at, z.local), :] = wire[pl.ds(start, z.local), :].astype(jnp.bfloat16)

        loop(z.pairs, one, min(8, z.pairs))


def block_rows(z, ref, index):
    return ref[pl.ds(pl.multiple_of(index * z.block, z.block), z.block), :]


def pair_rows(z, pair):
    return pl.ds(pl.multiple_of(pair * z.block, z.block), z.block)


def place(z, piece_refs, hid, pair, ref):
    for d, piece in enumerate(piece_refs):
        src = source(hid, d, z.hidden)
        start = pl.multiple_of(pair * z.block + src * z.local, z.local)
        ref[pl.ds(start, z.local), :] = piece[
            pl.ds(pl.multiple_of(pair * z.local, z.local), z.local), :
        ]


def consume(z, weight_ref, values, pair):
    parts = [dot(block_rows(z, weight_ref, g * z.pairs + pair), values) for g in range(z.groups)]
    return pick(parts, lane_group(z, z.block))


def loop(count, body, unroll=UNROLL):
    def step(i, carry):
        body(i)
        return carry

    lax.fori_loop(0, count, step, 0, unroll=unroll)


def whole(shape):
    return pl.BlockSpec(shape, lambda i, s: tuple(0 for _ in shape))


ANY = pl.BlockSpec(memory_space=pl.ANY)


class Order:
    token = None


def call(
    body, scalars, args, in_specs, outs, out_specs, scratch=(), aliases=None, flops=0, grant=12
):
    size = lambda a: math.prod(a.shape) * a.dtype.itemsize
    moved = sum(size(a) for a, s in zip(args, in_specs) if s is not ANY)
    moved += sum(size(o) for o in outs)
    n_in, n_out = len(args), len(outs)

    def ordered(s, *refs):
        body(s, *refs[:n_in], *refs[n_in + 1 : n_in + 1 + n_out], *refs[n_in + n_out + 2 :])

    token = Order.token
    *got, Order.token = pl.pallas_call(
        ordered,
        grid_spec=pltpu.PrefetchScalarGridSpec(
            num_scalar_prefetch=1,
            grid=(1,),
            in_specs=[*in_specs, ANY],
            out_specs=[*out_specs, ANY],
            scratch_shapes=list(scratch),
        ),
        out_shape=[*outs, jax.ShapeDtypeStruct(token.shape, token.dtype)],
        input_output_aliases={**(aliases or {}), n_in + 1: n_out},
        cost_estimate=pl.CostEstimate(flops=flops, bytes_accessed=moved, transcendentals=0),
        compiler_params=pltpu.CompilerParams(vmem_limit_bytes=grant * 2**20),
    )(scalars, *args, token)
    return got


def bf16(*shape):
    return jax.ShapeDtypeStruct(shape, jnp.bfloat16)


def f32(*shape):
    return jax.ShapeDtypeStruct(shape, jnp.float32)


def shuffle_matrix(z):
    row = lax.broadcasted_iota(jnp.int32, (z.block, z.block), 0)
    col = lax.broadcasted_iota(jnp.int32, (z.block, z.block), 1)
    g = row // z.picked
    rest = row - g * z.picked
    h = rest // z.pairs
    pair = rest - h * z.pairs
    return (col == h * z.local + g * z.pairs + pair).astype(jnp.bfloat16)


def unit_matrix(z):
    row = lax.broadcasted_iota(jnp.int32, (z.block, z.block), 0)
    col = lax.broadcasted_iota(jnp.int32, (z.block, z.block), 1)
    return (col == row).astype(jnp.bfloat16)


def prepare(z, scalars, pieces, forms):
    def body(s, *refs):
        ins, outs = refs[: z.tok], refs[z.tok :]
        unit, shuffle = unit_matrix(z), shuffle_matrix(z)
        for d, piece in enumerate(ins):
            first = source(s[3], d, z.tok) * z.share

            def one(i):
                w = block_rows(z, piece, i)
                at = pair_rows(z, first + i)
                for form, out in zip(forms, outs):
                    if form == "n":
                        out[at, :] = w
                    else:
                        left = shuffle if "p" in form else unit
                        out[at, :] = dot(left, w, NT if "t" in form else NN).astype(jnp.bfloat16)

            loop(z.share, one)

    size = z.local * z.block
    return call(
        body, scalars, pieces,
        [whole((z.share * z.block, z.block))] * z.tok,
        [bf16(size, z.block)] * len(forms), [whole((size, z.block))] * len(forms),
    )


def piece_specs(z):
    return [whole((z.piece, z.block))] * z.hidden


def piece_shapes(z):
    return [bf16(z.piece, z.block)] * z.hidden


def wire_scratch(z):
    return pltpu.VMEM((z.picked * z.pitch, z.block), jnp.float32)


def matmul_flops(z, count):
    return 2 * count * z.local * z.block**3


def first_mid(z, scalars, m, inputs, weight):
    def body(s, x, w, *rest):
        pieces, wire = rest[: z.hidden], rest[z.hidden]

        def one(b):
            cols = pl.ds(pl.multiple_of(b * z.block, z.block), z.block)
            xb = x[:, cols]
            values = jnp.concatenate([xb] * z.groups, axis=0)
            full = dot(block_rows(z, w, b), values, NT)
            parts = [full[g * z.picked : (g + 1) * z.picked] for g in range(z.groups)]
            wire[pl.ds(b, z.picked, stride=z.pitch), :] = pick(parts, lane_group(z, z.picked))

        loop(z.local, one)
        send_pieces(z, wire, s[0], pieces)

    return call(
        body, scalars, [inputs, weight],
        [pl.BlockSpec((z.tokens, z.width), lambda i, s: (m, 0)), whole(weight.shape)],
        piece_shapes(z), piece_specs(z), [wire_scratch(z)], flops=matmul_flops(z, 1),
    )


def forward_wide(z, scalars, pieces, weight):
    def body(s, *refs):
        ins, w = refs[: z.hidden], refs[z.hidden]
        fw, act, deriv = refs[z.hidden + 1 :]

        def one(pair):
            place(z, ins, s[0], pair, fw)
            at = pair_rows(z, pair)
            a, d = gelu_parts(consume(z, w, fw[at, :], pair))
            act[at, :] = a.astype(jnp.bfloat16)
            deriv[at, :] = d.astype(jnp.bfloat16)

        loop(z.pairs, one)

    return call(
        body, scalars, [*pieces, weight],
        piece_specs(z) + [whole(weight.shape)],
        [bf16(z.rows, z.block)] * 3, [whole((z.rows, z.block))] * 3, flops=matmul_flops(z, 1),
    )


def second_mid(z, scalars, act, weight):
    def body(s, a, w, *rest):
        pieces, wire = rest[: z.hidden], rest[z.hidden]

        def one(pair):
            values = a[pair_rows(z, pair), :].astype(jnp.float32)
            for g, repeated in enumerate(spread(z, values)):
                index = g * z.pairs + pair
                produce(z, wire, block_rows(z, w, index), repeated, index)

        loop(z.pairs, one)
        send_pieces(z, wire, s[0], pieces)

    return call(
        body, scalars, [act, weight],
        [whole(act.shape), whole(weight.shape)],
        piece_shapes(z), piece_specs(z), [wire_scratch(z)], flops=matmul_flops(z, 1),
    )


def saved_spec(z):
    return pl.BlockSpec((1, z.rows, z.block), lambda i, s: (s[2], 0, 0))


def backward_in(z, scalars, k, top, incoming, weight, gy_saved):
    has_top = k < z.micro

    def body(s, *refs):
        if has_top:
            t, inc, w, _, *rest = refs
        else:
            inc, w, _, *rest = refs
        gy, rest = rest[0], rest[1:]
        if has_top:
            plain, rest = rest[0], rest[1:]
        pieces, wire = rest[: z.hidden], rest[z.hidden]

        if has_top:

            @pl.when(s[1] == 0)
            def _():
                unit = unit_matrix(z)

                def one(pair):
                    parts = []
                    for g in range(z.groups):
                        start = pl.multiple_of((g * z.pairs + pair) * z.block, z.block)
                        parts.append(t[:, pl.ds(start, z.block)])
                    values = jnp.concatenate(parts, axis=0)
                    plain[pair_rows(z, pair), :] = dot(unit, values, NT).astype(jnp.bfloat16)

                loop(z.pairs, one)

            @pl.when(s[1] != 0)
            def _():
                plain[...] = inc[...]

            held = plain
        else:
            held = inc

        def one(pair):
            at = pair_rows(z, pair)
            value = held[at, :]
            gy[0, at, :] = value
            for g, repeated in enumerate(spread(z, value.astype(jnp.float32))):
                index = g * z.pairs + pair
                produce(z, wire, block_rows(z, w, index), repeated, index)

        loop(z.pairs, one)
        send_pieces(z, wire, s[0], pieces)

    flat = (z.rows, z.block)
    args = [incoming, weight, gy_saved]
    specs = [whole(flat), whole(weight.shape), ANY]
    if has_top:
        args = [top] + args
        specs = [pl.BlockSpec((z.tokens, z.width), lambda i, s: (k, 0))] + specs
    outs = [jax.ShapeDtypeStruct(gy_saved.shape, gy_saved.dtype)]
    out_specs = [saved_spec(z)]
    if has_top:
        outs.append(bf16(*flat))
        out_specs.append(whole(flat))
    got = call(
        body, scalars, args, specs,
        outs + piece_shapes(z), out_specs + piece_specs(z), [wire_scratch(z)],
        aliases={len(args): 0}, flops=matmul_flops(z, 1),
    )
    if has_top:
        return got[0], got[1], got[2:]
    return got[0], incoming, got[1:]


def backward_wide(z, scalars, pieces, weight_rs, weight_lf, options, gw_saved, gp_saved):
    def body(s, *refs):
        ins, refs = refs[: z.hidden], refs[z.hidden :]
        rs, lf, refs = refs[0], refs[1], refs[2:]
        derivs, refs = refs[: len(options)], refs[len(options) + 2 :]
        gw, gp, refs = refs[0], refs[1], refs[2:]
        out, (wire, deriv, sem) = refs[: z.hidden], refs[z.hidden :]
        if len(options) == 1:
            pltpu.make_async_copy(derivs[0], deriv, sem).start()
        else:
            first, last = options[0][0], options[-1][0]
            for (where, _), ref in zip(options, derivs):
                here = s[1] == where
                if where == first:
                    here = s[1] <= where
                elif where == last:
                    here = s[1] >= where

                @pl.when(here)
                def _():
                    pltpu.make_async_copy(ref, deriv, sem).start()

        loop(z.pairs, lambda pair: place(z, ins, s[0], pair, gw.at[0]))
        pltpu.make_async_copy(derivs[0], deriv, sem).wait()

        def one(pair):
            at = pair_rows(z, pair)
            grad = consume(z, rs, gw[0, at, :], pair) * deriv[at, :].astype(jnp.float32)
            rounded = grad.astype(jnp.bfloat16)
            gp[0, at, :] = rounded

        def two(pair):
            values = gp[0, pair_rows(z, pair), :].astype(jnp.float32)
            for g, repeated in enumerate(spread(z, values)):
                index = g * z.pairs + pair
                produce(z, wire, block_rows(z, lf, index), repeated, index)

        loop(z.pairs, one)
        loop(z.pairs, two)
        send_pieces(z, wire, s[0], out)

    args = [*pieces, weight_rs, weight_lf, *[d for _, d in options], gw_saved, gp_saved]
    first = len(args) - 1
    got = call(
        body, scalars, args,
        piece_specs(z) + [whole(weight_rs.shape)] * 2 + [ANY] * (len(options) + 2),
        [jax.ShapeDtypeStruct(a.shape, a.dtype) for a in (gw_saved, gp_saved)] + piece_shapes(z),
        [saved_spec(z)] * 2 + piece_specs(z),
        [wire_scratch(z), pltpu.VMEM((z.rows, z.block), jnp.bfloat16), pltpu.SemaphoreType.DMA],
        aliases={first: 0, first + 1: 1}, flops=matmul_flops(z, 2),
    )
    return got[0], got[1], got[2:]


def backward_out(z, scalars, pieces, weight, gy, gn_saved, adj_saved):
    def body(s, *refs):
        ins, (w, g_ref, _, _, gn, adj, nxt) = refs[: z.hidden], refs[z.hidden :]

        def one(pair):
            at = pair_rows(z, pair)
            place(z, ins, s[0], pair, gn.at[0])
            grad = consume(z, w, gn[0, at, :], pair)
            value = (g_ref[at, :].astype(jnp.float32) + grad).astype(jnp.bfloat16)
            adj[0, at, :] = value
            nxt[at, :] = value

        loop(z.pairs, one)

    args = [*pieces, weight, gy, gn_saved, adj_saved]
    flat = (z.rows, z.block)
    return call(
        body, scalars, args,
        piece_specs(z) + [whole(weight.shape), whole(flat), ANY, ANY],
        [jax.ShapeDtypeStruct(a.shape, a.dtype) for a in (gn_saved, adj_saved)] + [bf16(*flat)],
        [saved_spec(z)] * 2 + [whole(flat)],
        aliases={len(args) - 1: 0, len(args): 1}, flops=matmul_flops(z, 1),
    )


def all_saved(z):
    return pl.BlockSpec((z.micro, z.rows, z.block), lambda i, s: (0, 0, 0))


def gradient(z, scalars, left, right, kind, shared):
    right_args = {"saved": [right], "rows": [right]}.get(kind)
    if kind == "list":
        right_args = list(right)
    elif kind == "pieces":
        right_args = [p for group in right for p in group]
    count = z.share * z.block

    def body(s, l, *refs):
        ins, refs = refs[: len(right_args)], refs[len(right_args) :]
        outs = refs[: z.tok]
        if kind == "pieces":
            held = refs[z.tok]
            for m in range(z.micro):
                group = ins[m * z.hidden : (m + 1) * z.hidden]
                loop(z.pairs, lambda pair: place(z, group, s[0], pair, held.at[m]))

        group_of = lane_group(z, z.block)
        for d, out in enumerate(outs):
            owner = partner(s[3], d, z.tok) * z.share

            def one(i):
                index = owner + i
                g = lax.div(index, z.pairs)
                pair = index - g * z.pairs
                at = pair_rows(z, pair)
                total = None
                for m in range(z.micro):
                    a = l[m, at, :]
                    a = jnp.where(group_of == g, a, jnp.zeros_like(a))
                    if kind == "rows":
                        rows = []
                        for q in range(z.groups):
                            start = pl.multiple_of((q * z.pairs + pair) * z.block, z.block)
                            rows.append(
                                ins[0][m * z.tokens : (m + 1) * z.tokens, pl.ds(start, z.block)]
                            )
                        term = dot(a, jnp.concatenate(rows, axis=0))
                    else:
                        if kind == "saved":
                            b = ins[0][m, at, :]
                        elif kind == "list":
                            b = ins[m][at, :]
                        else:
                            b = held[m, at, :]
                        term = dot(a, b, NT)
                    total = term if total is None else total + term
                out[pair_rows(z, i), :] = total.astype(out.dtype)

            loop(z.share, one)

    if kind == "saved":
        specs = [all_saved(z)]
    else:
        specs = [whole(a.shape) for a in right_args]
    scratch = []
    if kind == "pieces":
        scratch = [pltpu.VMEM((z.micro, z.rows, z.block), jnp.bfloat16)]
    got = call(
        body, scalars, [left, *right_args], [all_saved(z)] + specs,
        [f32(count, z.block)] + [bf16(count, z.block)] * (z.tok - 1),
        [whole((count, z.block))] * z.tok, scratch, flops=matmul_flops(z, z.micro), grant=28,
    )
    received = exchange(got, "tok")
    total = received[0]
    for other in received[1:]:
        total = total + other.astype(jnp.float32)
    return (total * shared).reshape(1, z.share, z.block, z.block)


def token_rows(z, scalars, saved):
    def body(s, a, out):
        for m in range(z.micro):

            def one(pair):
                turned = a[m, pair_rows(z, pair), :].astype(jnp.float32).T.astype(jnp.bfloat16)
                for g in range(z.groups):
                    start = pl.multiple_of((g * z.pairs + pair) * z.block, z.block)
                    out[m * z.tokens : (m + 1) * z.tokens, pl.ds(start, z.block)] = turned[
                        g * z.tokens : (g + 1) * z.tokens
                    ]

            loop(z.pairs, one)

    return call(
        body, scalars, [saved], [all_saved(z)],
        [bf16(z.tok_rows, z.width)], [whole((z.tok_rows, z.width))], grant=28,
    )[0]


def on_device(section_inputs, top_adjoint, right_first, left_first, right_second, left_second):
    sections = lax.axis_size("section")
    token_count = lax.axis_size("tok")
    hidden_count = lax.axis_size("hidden")
    _, share, block, _ = right_first.shape
    inputs = section_inputs[0]
    tok_rows = inputs.shape[0]
    z = Shape(hidden_count, token_count, share * token_count, block, tok_rows)
    hid = lax.axis_index("hidden")
    depth = sections - 1 - lax.axis_index("section")
    tok = lax.axis_index("tok")
    shared = 1.0 / math.sqrt(tok_rows * token_count)

    def scalars_of(slot):
        return jnp.stack([hid, depth, slot, tok]).astype(jnp.int32)

    base = scalars_of(jnp.int32(0))

    Order.token = jnp.zeros((8, 128), jnp.float32)
    own_rf, own_lf, own_rs, own_ls = (
        w.reshape(share * block, block)
        for w in (right_first, left_first, right_second, left_second)
    )
    all_rf = exchange([own_rf] * token_count, "tok")
    *all_rf, own_lf, own_ls = lax.optimization_barrier((*all_rf, own_lf, own_ls))
    all_ls = exchange([own_ls] * token_count, "tok")
    all_lf = exchange([own_lf] * token_count, "tok")
    *all_lf, own_rs = lax.optimization_barrier((*all_lf, own_rs))
    all_rs = exchange([own_rs] * token_count, "tok")

    saved = jnp.zeros((z.micro + 1, z.rows, z.block), jnp.bfloat16)
    kept = {name: saved for name in ("gy", "gw", "gp", "gn", "adj")}
    zero = jnp.zeros((z.rows, z.block), jnp.bfloat16)
    ticks = z.micro + SKEW * (sections - 1)
    arrivals, sent, adjoint, mids = {}, {}, {}, {}
    wides, acts, derivs, seconds = [], [], [], []
    scalars = []
    for k in range(ticks):
        micro = k - SKEW * depth
        active = jnp.logical_and(micro >= 0, micro < z.micro)
        scalars.append(scalars_of(jnp.where(active, micro, z.micro)))

    def mid_stage(m):
        if m < z.micro:
            pieces = first_mid(z, base, m, inputs, rf_mid)
            mids[m] = exchange(pieces, "hidden")

    def wide_stage(m):
        if m < z.micro:
            wide, act, deriv = forward_wide(z, base, mids.pop(m), lf_mid)
            wides.append(wide)
            acts.append(act)
            derivs.append(deriv)

    def second_stage(m):
        if 0 <= m < z.micro:
            pieces = second_mid(z, base, acts[m], rs_mid)
            seconds.append(exchange(pieces, "hidden"))

    def in_stage(k):
        incoming = arrivals.pop(k, zero)
        kept["gy"], adjoint[k], pieces = backward_in(
            z, scalars[k], k, top_adjoint, incoming, ls_in, kept["gy"]
        )
        sent[k] = exchange(pieces, "hidden")

    def back_stage(k):
        options = [
            (c, derivs[k - SKEW * c])
            for c in range(sections)
            if 0 <= k - SKEW * c < z.micro
        ]
        kept["gw"], kept["gp"], pieces = backward_wide(
            z, scalars[k], sent[k], rs_back, lf_back, options, kept["gw"], kept["gp"]
        )
        sent[k] = exchange(pieces, "hidden")

    def out_stage(k):
        kept["gn"], kept["adj"], nxt = backward_out(
            z, scalars[k], sent.pop(k), rf_out, adjoint.pop(k), kept["gn"], kept["adj"]
        )
        if k + SKEW < ticks:
            route = [(i, i - 1) for i in range(1, sections)]
            arrivals[k + SKEW] = lax.ppermute(nxt, "section", route)

    rf_mid, rf_out = prepare(z, base, all_rf, ("p", "t"))
    mid_stage(0)
    mid_stage(1)
    (ls_in,) = prepare(z, base, all_ls, ("tp",))
    in_stage(0)
    lf_mid, lf_back = prepare(z, base, all_lf, ("n", "tp"))
    wide_stage(0)
    mid_stage(2)
    (rs_back,) = prepare(z, base, all_rs, ("t",))
    back_stage(0)
    (rs_mid,) = prepare(z, base, all_rs, ("p",))
    wide_stage(1)
    for k in range(1, ticks):
        in_stage(k)
        out_stage(k - 1)
        if k == ticks - 1:
            grad_ls = gradient(z, base, kept["gy"], seconds, "pieces", shared)
        mid_stage(k + 2)
        second_stage(k - (ticks - 1 - z.micro))
        back_stage(k)
        wide_stage(k + 1)
    grad_rs = gradient(z, base, kept["gw"], acts, "list", shared)
    grad_lf = gradient(z, base, kept["gp"], wides, "list", shared)
    out_stage(ticks - 1)
    grad_rf = gradient(z, base, kept["gn"], inputs, "rows", shared)
    adjoints = token_rows(z, base, kept["adj"])
    return adjoints[None], grad_rf, grad_lf, grad_rs, grad_ls


def solution(mesh):
    blocks = P("section", ("hidden", "tok"), None, None)
    rows = P("section", "tok", "hidden")

    def step(*arrays):
        mapped = jax.shard_map(
            on_device,
            mesh=mesh,
            in_specs=(rows, P("tok", "hidden"), blocks, blocks, blocks, blocks),
            out_specs=(rows, blocks, blocks, blocks, blocks),
            check_vma=False,
        )
        return mapped(*arrays)

    return step
```

```python
import math

import jax
import jax.numpy as jnp
from jax import lax
from jax.experimental import pallas as pl
from jax.experimental.pallas import tpu as pltpu
from jax.sharding import PartitionSpec as P


GROUPS = 2
SKEW = 2
UNROLL = 8


gelu_coef = 0.7978845608028654
NT = (((1,), (1,)), ((), ()))
NN = (((1,), (0,)), ((), ()))


def gelu_parts(preact):
    inner_arg = gelu_coef * (preact + 0.044715 * preact * preact * preact)
    squashed = jnp.tanh(inner_arg)
    activation = 0.5 * preact * (1.0 + squashed)
    derivative = 0.5 * (1.0 + squashed) + 0.5 * preact * (1.0 - squashed * squashed) * gelu_coef * (
        1.0 + 3.0 * 0.044715 * preact * preact
    )
    return (activation, derivative)


def dot(a, b, dims=NN):
    return lax.dot_general(a, b, dims, preferred_element_type=jnp.float32)


def partner(me, distance, count):
    if count & (count - 1) == 0:
        return me ^ distance
    return lax.rem(me + distance, count)


def source(me, distance, count):
    if count & (count - 1) == 0:
        return me ^ distance
    return lax.rem(me + count - distance, count)


def exchange(pieces, axis):
    count = len(pieces)
    out = [pieces[0]]
    for distance in range(1, count):
        if count & (count - 1) == 0:
            route = [(i, i ^ distance) for i in range(count)]
        else:
            route = [(i, (i + distance) % count) for i in range(count)]
        out.append(lax.ppermute(pieces[distance], axis, route))
    return out


class Shape:
    def __init__(self, hidden_count, token_count, local_count, block, tok_rows):
        self.hidden = hidden_count
        self.tok = token_count
        self.local = local_count
        self.block = block
        self.groups = GROUPS
        self.pairs = local_count // GROUPS
        self.tokens = block // GROUPS
        self.micro = tok_rows // self.tokens
        self.share = local_count // token_count
        self.rows = self.pairs * block
        self.picked = block // GROUPS
        self.piece = self.pairs * local_count
        self.pitch = local_count + 8
        self.tok_rows = tok_rows
        self.width = local_count * block


def lane_group(z, rows):
    return lax.broadcasted_iota(jnp.int32, (rows, z.block), 1) // z.tokens


def pick(parts, group):
    out = parts[0]
    for g in range(1, len(parts)):
        out = jnp.where(group == g, parts[g], out)
    return out


def spread(z, values):
    turned = [values] + [
        pltpu.roll(values, s * z.tokens, 1) for s in range(1, z.groups)
    ]
    group = lane_group(z, values.shape[0])
    return [
        pick([turned[(q - g) % z.groups] for q in range(z.groups)], group).astype(jnp.bfloat16)
        for g in range(z.groups)
    ]


def produce(z, wire, weight, values, index):
    full = dot(weight, values)
    parts = [full[g * z.picked : (g + 1) * z.picked] for g in range(z.groups)]
    wire[pl.ds(index, z.picked, stride=z.pitch), :] = pick(parts, lane_group(z, z.picked))


def send_pieces(z, wire, hid, piece_refs):
    for d, ref in enumerate(piece_refs):
        first = partner(hid, d, z.hidden) * z.pairs

        def one(pair):
            start = pl.multiple_of((first + pair) * z.pitch, 8)
            at = pl.multiple_of(pair * z.local, z.local)
            ref[pl.ds(at, z.local), :] = wire[pl.ds(start, z.local), :].astype(jnp.bfloat16)

        loop(z.pairs, one, min(8, z.pairs))


def block_rows(z, ref, index):
    return ref[pl.ds(pl.multiple_of(index * z.block, z.block), z.block), :]


def pair_rows(z, pair):
    return pl.ds(pl.multiple_of(pair * z.block, z.block), z.block)


def place(z, piece_refs, hid, pair, ref):
    for d, piece in enumerate(piece_refs):
        src = source(hid, d, z.hidden)
        start = pl.multiple_of(pair * z.block + src * z.local, z.local)
        ref[pl.ds(start, z.local), :] = piece[
            pl.ds(pl.multiple_of(pair * z.local, z.local), z.local), :
        ]


def consume(z, weight_ref, values, pair):
    parts = [dot(block_rows(z, weight_ref, g * z.pairs + pair), values) for g in range(z.groups)]
    return pick(parts, lane_group(z, z.block))


def loop(count, body, unroll=UNROLL):
    def step(i, carry):
        body(i)
        return carry

    lax.fori_loop(0, count, step, 0, unroll=unroll)


def whole(shape):
    return pl.BlockSpec(shape, lambda i, s: tuple(0 for _ in shape))


ANY = pl.BlockSpec(memory_space=pl.ANY)


class Order:
    token = None


def call(
    body, scalars, args, in_specs, outs, out_specs, scratch=(), aliases=None, flops=0, grant=12
):
    size = lambda a: math.prod(a.shape) * a.dtype.itemsize
    moved = sum(size(a) for a, s in zip(args, in_specs) if s is not ANY)
    moved += sum(size(o) for o in outs)
    n_in, n_out = len(args), len(outs)

    def ordered(s, *refs):
        body(s, *refs[:n_in], *refs[n_in + 1 : n_in + 1 + n_out], *refs[n_in + n_out + 2 :])

    token = Order.token
    *got, Order.token = pl.pallas_call(
        ordered,
        grid_spec=pltpu.PrefetchScalarGridSpec(
            num_scalar_prefetch=1,
            grid=(1,),
            in_specs=[*in_specs, ANY],
            out_specs=[*out_specs, ANY],
            scratch_shapes=list(scratch),
        ),
        out_shape=[*outs, jax.ShapeDtypeStruct(token.shape, token.dtype)],
        input_output_aliases={**(aliases or {}), n_in + 1: n_out},
        cost_estimate=pl.CostEstimate(flops=flops, bytes_accessed=moved, transcendentals=0),
        compiler_params=pltpu.CompilerParams(vmem_limit_bytes=grant * 2**20),
    )(scalars, *args, token)
    return got


def bf16(*shape):
    return jax.ShapeDtypeStruct(shape, jnp.bfloat16)


def f32(*shape):
    return jax.ShapeDtypeStruct(shape, jnp.float32)


def shuffle_matrix(z):
    row = lax.broadcasted_iota(jnp.int32, (z.block, z.block), 0)
    col = lax.broadcasted_iota(jnp.int32, (z.block, z.block), 1)
    g = row // z.picked
    rest = row - g * z.picked
    h = rest // z.pairs
    pair = rest - h * z.pairs
    return (col == h * z.local + g * z.pairs + pair).astype(jnp.bfloat16)


def unit_matrix(z):
    row = lax.broadcasted_iota(jnp.int32, (z.block, z.block), 0)
    col = lax.broadcasted_iota(jnp.int32, (z.block, z.block), 1)
    return (col == row).astype(jnp.bfloat16)


def prepare(z, scalars, pieces, forms):
    def body(s, *refs):
        ins, outs = refs[: z.tok], refs[z.tok :]
        unit, shuffle = unit_matrix(z), shuffle_matrix(z)
        for d, piece in enumerate(ins):
            first = source(s[3], d, z.tok) * z.share

            def one(i):
                w = block_rows(z, piece, i)
                at = pair_rows(z, first + i)
                for form, out in zip(forms, outs):
                    if form == "n":
                        out[at, :] = w
                    else:
                        left = shuffle if "p" in form else unit
                        out[at, :] = dot(left, w, NT if "t" in form else NN).astype(jnp.bfloat16)

            loop(z.share, one)

    size = z.local * z.block
    return call(
        body, scalars, pieces,
        [whole((z.share * z.block, z.block))] * z.tok,
        [bf16(size, z.block)] * len(forms), [whole((size, z.block))] * len(forms),
    )


def piece_specs(z):
    return [whole((z.piece, z.block))] * z.hidden


def piece_shapes(z):
    return [bf16(z.piece, z.block)] * z.hidden


def wire_scratch(z):
    return pltpu.VMEM((z.picked * z.pitch, z.block), jnp.float32)


def matmul_flops(z, count):
    return 2 * count * z.local * z.block**3


def first_mid(z, scalars, m, inputs, weight):
    def body(s, x, w, *rest):
        pieces, wire = rest[: z.hidden], rest[z.hidden]

        def one(b):
            cols = pl.ds(pl.multiple_of(b * z.block, z.block), z.block)
            xb = x[:, cols]
            values = jnp.concatenate([xb] * z.groups, axis=0)
            full = dot(block_rows(z, w, b), values, NT)
            parts = [full[g * z.picked : (g + 1) * z.picked] for g in range(z.groups)]
            wire[pl.ds(b, z.picked, stride=z.pitch), :] = pick(parts, lane_group(z, z.picked))

        loop(z.local, one)
        send_pieces(z, wire, s[0], pieces)

    return call(
        body, scalars, [inputs, weight],
        [pl.BlockSpec((z.tokens, z.width), lambda i, s: (m, 0)), whole(weight.shape)],
        piece_shapes(z), piece_specs(z), [wire_scratch(z)], flops=matmul_flops(z, 1),
    )


def forward_wide(z, scalars, pieces, weight):
    def body(s, *refs):
        ins, w = refs[: z.hidden], refs[z.hidden]
        fw, act, deriv = refs[z.hidden + 1 :]

        def one(pair):
            place(z, ins, s[0], pair, fw)
            at = pair_rows(z, pair)
            a, d = gelu_parts(consume(z, w, fw[at, :], pair))
            act[at, :] = a.astype(jnp.bfloat16)
            deriv[at, :] = d.astype(jnp.bfloat16)

        loop(z.pairs, one)

    return call(
        body, scalars, [*pieces, weight],
        piece_specs(z) + [whole(weight.shape)],
        [bf16(z.rows, z.block)] * 3, [whole((z.rows, z.block))] * 3, flops=matmul_flops(z, 1),
    )


def second_mid(z, scalars, act, weight):
    def body(s, a, w, *rest):
        pieces, wire = rest[: z.hidden], rest[z.hidden]

        def one(pair):
            values = a[pair_rows(z, pair), :].astype(jnp.float32)
            for g, repeated in enumerate(spread(z, values)):
                index = g * z.pairs + pair
                produce(z, wire, block_rows(z, w, index), repeated, index)

        loop(z.pairs, one)
        send_pieces(z, wire, s[0], pieces)

    return call(
        body, scalars, [act, weight],
        [whole(act.shape), whole(weight.shape)],
        piece_shapes(z), piece_specs(z), [wire_scratch(z)], flops=matmul_flops(z, 1),
    )


def saved_shape(z):
    return bf16(z.micro + 1, z.rows, z.block)


def chained(arrays, first):
    given = [a for a in arrays if a is not None]
    return given, [ANY] * len(given), {first + 1 + i: i for i in range(len(given))}


def saved_spec(z):
    return pl.BlockSpec((1, z.rows, z.block), lambda i, s: (s[2], 0, 0))


def backward_in(z, scalars, k, top, incoming, weight, gy_saved):
    has_top = k < z.micro

    def body(s, *refs):
        if has_top:
            t, inc, w, *rest = refs
        else:
            inc, w, *rest = refs
        rest = rest[len(given) :]
        gy, rest = rest[0], rest[1:]
        if has_top:
            plain, rest = rest[0], rest[1:]
        pieces, wire = rest[: z.hidden], rest[z.hidden]

        if has_top:

            @pl.when(s[1] == 0)
            def _():
                unit = unit_matrix(z)

                def one(pair):
                    parts = []
                    for g in range(z.groups):
                        start = pl.multiple_of((g * z.pairs + pair) * z.block, z.block)
                        parts.append(t[:, pl.ds(start, z.block)])
                    values = jnp.concatenate(parts, axis=0)
                    plain[pair_rows(z, pair), :] = dot(unit, values, NT).astype(jnp.bfloat16)

                loop(z.pairs, one)

            @pl.when(s[1] != 0)
            def _():
                plain[...] = inc[...]

            held = plain
        else:
            held = inc

        def one(pair):
            at = pair_rows(z, pair)
            value = held[at, :]
            gy[0, at, :] = value
            for g, repeated in enumerate(spread(z, value.astype(jnp.float32))):
                index = g * z.pairs + pair
                produce(z, wire, block_rows(z, w, index), repeated, index)

        loop(z.pairs, one)
        send_pieces(z, wire, s[0], pieces)

    flat = (z.rows, z.block)
    args = [incoming, weight]
    specs = [whole(flat), whole(weight.shape)]
    if has_top:
        args = [top] + args
        specs = [pl.BlockSpec((z.tokens, z.width), lambda i, s: (k, 0))] + specs
    given, given_specs, aliases = chained([gy_saved], len(args))
    args, specs = args + given, specs + given_specs
    outs = [saved_shape(z)]
    out_specs = [saved_spec(z)]
    if has_top:
        outs.append(bf16(*flat))
        out_specs.append(whole(flat))
    got = call(
        body, scalars, args, specs,
        outs + piece_shapes(z), out_specs + piece_specs(z), [wire_scratch(z)],
        aliases=aliases, flops=matmul_flops(z, 1),
    )
    if has_top:
        return got[0], got[1], got[2:]
    return got[0], incoming, got[1:]


def backward_wide(z, scalars, pieces, weight_rs, weight_lf, options, gw_saved, gp_saved):
    def body(s, *refs):
        ins, refs = refs[: z.hidden], refs[z.hidden :]
        rs, lf, refs = refs[0], refs[1], refs[2:]
        derivs, refs = refs[: len(options)], refs[len(options) + len(given) :]
        gw, gp, refs = refs[0], refs[1], refs[2:]
        out, (wire, deriv, sem) = refs[: z.hidden], refs[z.hidden :]
        if len(options) == 1:
            pltpu.make_async_copy(derivs[0], deriv, sem).start()
        else:
            first, last = options[0][0], options[-1][0]
            for (where, _), ref in zip(options, derivs):
                here = s[1] == where
                if where == first:
                    here = s[1] <= where
                elif where == last:
                    here = s[1] >= where

                @pl.when(here)
                def _():
                    pltpu.make_async_copy(ref, deriv, sem).start()

        loop(z.pairs, lambda pair: place(z, ins, s[0], pair, gw.at[0]))
        pltpu.make_async_copy(derivs[0], deriv, sem).wait()

        def one(pair):
            at = pair_rows(z, pair)
            grad = consume(z, rs, gw[0, at, :], pair) * deriv[at, :].astype(jnp.float32)
            rounded = grad.astype(jnp.bfloat16)
            gp[0, at, :] = rounded

        def two(pair):
            values = gp[0, pair_rows(z, pair), :].astype(jnp.float32)
            for g, repeated in enumerate(spread(z, values)):
                index = g * z.pairs + pair
                produce(z, wire, block_rows(z, lf, index), repeated, index)

        loop(z.pairs, one)
        loop(z.pairs, two)
        send_pieces(z, wire, s[0], out)

    args = [*pieces, weight_rs, weight_lf, *[d for _, d in options]]
    given, given_specs, aliases = chained([gw_saved, gp_saved], len(args))
    args += given
    got = call(
        body, scalars, args,
        piece_specs(z) + [whole(weight_rs.shape)] * 2 + [ANY] * len(options) + given_specs,
        [saved_shape(z)] * 2 + piece_shapes(z),
        [saved_spec(z)] * 2 + piece_specs(z),
        [wire_scratch(z), pltpu.VMEM((z.rows, z.block), jnp.bfloat16), pltpu.SemaphoreType.DMA],
        aliases=aliases, flops=matmul_flops(z, 2),
    )
    return got[0], got[1], got[2:]


def backward_out(z, scalars, pieces, weight, gy, gn_saved, adj_saved):
    def body(s, *refs):
        ins, (w, g_ref, *rest) = refs[: z.hidden], refs[z.hidden :]
        gn, adj, nxt = rest[len(given) :]

        def one(pair):
            at = pair_rows(z, pair)
            place(z, ins, s[0], pair, gn.at[0])
            grad = consume(z, w, gn[0, at, :], pair)
            value = (g_ref[at, :].astype(jnp.float32) + grad).astype(jnp.bfloat16)
            adj[0, at, :] = value
            nxt[at, :] = value

        loop(z.pairs, one)

    args = [*pieces, weight, gy]
    given, given_specs, aliases = chained([gn_saved, adj_saved], len(args))
    args += given
    flat = (z.rows, z.block)
    return call(
        body, scalars, args,
        piece_specs(z) + [whole(weight.shape), whole(flat), *given_specs],
        [saved_shape(z)] * 2 + [bf16(*flat)],
        [saved_spec(z)] * 2 + [whole(flat)],
        aliases=aliases, flops=matmul_flops(z, 1),
    )


def all_saved(z):
    return pl.BlockSpec((z.micro, z.rows, z.block), lambda i, s: (0, 0, 0))


def gradient(z, scalars, left, right, kind, lo, hi, held=None, part=False):
    span = hi - lo
    right_args = [right]
    if kind == "list":
        right_args = list(right[lo:hi])
    elif kind == "pieces":
        right_args = [p for group in right[lo:hi] for p in group]
    before = [] if held is None else [held]
    count = (z.local if part else z.share) * z.block
    outputs = 1 if part else z.tok

    def body(s, l, *refs):
        ins, refs = refs[: len(right_args)], refs[len(right_args) :]
        base, refs = refs[: len(before)], refs[len(before) :]
        outs = refs[:outputs]
        if kind == "pieces":
            joined = refs[outputs]
            for m in range(span):
                group = ins[m * z.hidden : (m + 1) * z.hidden]
                loop(z.pairs, lambda pair: place(z, group, s[0], pair, joined.at[m]))

        group_of = lane_group(z, z.block)
        for d, out in enumerate(outs):
            owner = 0 if part else partner(s[3], d, z.tok) * z.share

            def one(i):
                index = owner + i
                g = lax.div(index, z.pairs)
                pair = index - g * z.pairs
                at = pair_rows(z, pair)
                total = base[0][pair_rows(z, index), :] if base else None
                for m in range(span):
                    a = l[m, at, :]
                    a = jnp.where(group_of == g, a, jnp.zeros_like(a))
                    if kind == "rows":
                        rows = []
                        for q in range(z.groups):
                            start = pl.multiple_of((q * z.pairs + pair) * z.block, z.block)
                            first = (lo + m) * z.tokens
                            rows.append(ins[0][first : first + z.tokens, pl.ds(start, z.block)])
                        term = dot(a, jnp.concatenate(rows, axis=0))
                    else:
                        b = joined[m, at, :] if kind == "pieces" else ins[m][at, :]
                        term = dot(a, b, NT)
                    total = term if total is None else total + term
                out[pair_rows(z, i), :] = total.astype(out.dtype)

            loop(z.local if part else z.share, one)

    args = [left, *right_args, *before]
    specs = [pl.BlockSpec((span, z.rows, z.block), lambda i, s: (lo // span, 0, 0))]
    specs += [whole(a.shape) for a in args[1:]]
    scratch = []
    if kind == "pieces":
        scratch = [pltpu.VMEM((span, z.rows, z.block), jnp.bfloat16)]
    outs = [f32(count, z.block)] + [bf16(count, z.block)] * (outputs - 1)
    return call(
        body, scalars, args, specs, outs, [whole((count, z.block))] * outputs,
        scratch, flops=matmul_flops(z, span), grant=28,
    )


def finish(z, got, shared):
    received = exchange(got, "tok")
    total = received[0]
    for other in received[1:]:
        total = total + other.astype(jnp.float32)
    return (total * shared).reshape(1, z.share, z.block, z.block)


def token_rows(z, scalars, saved):
    def body(s, a, out):
        for m in range(z.micro):

            def one(pair):
                turned = a[m, pair_rows(z, pair), :].astype(jnp.float32).T.astype(jnp.bfloat16)
                for g in range(z.groups):
                    start = pl.multiple_of((g * z.pairs + pair) * z.block, z.block)
                    out[m * z.tokens : (m + 1) * z.tokens, pl.ds(start, z.block)] = turned[
                        g * z.tokens : (g + 1) * z.tokens
                    ]

            loop(z.pairs, one)

    return call(
        body, scalars, [saved], [all_saved(z)],
        [bf16(z.tok_rows, z.width)], [whole((z.tok_rows, z.width))], grant=28,
    )[0]


def on_device(section_inputs, top_adjoint, right_first, left_first, right_second, left_second):
    sections = lax.axis_size("section")
    token_count = lax.axis_size("tok")
    hidden_count = lax.axis_size("hidden")
    _, share, block, _ = right_first.shape
    inputs = section_inputs[0]
    tok_rows = inputs.shape[0]
    z = Shape(hidden_count, token_count, share * token_count, block, tok_rows)
    hid = lax.axis_index("hidden")
    depth = sections - 1 - lax.axis_index("section")
    tok = lax.axis_index("tok")
    shared = 1.0 / math.sqrt(tok_rows * token_count)

    def scalars_of(slot):
        return jnp.stack([hid, depth, slot, tok]).astype(jnp.int32)

    base = scalars_of(jnp.int32(0))

    Order.token = jnp.zeros((8, 128), jnp.float32)
    own_rf, own_lf, own_rs, own_ls = (
        w.reshape(share * block, block)
        for w in (right_first, left_first, right_second, left_second)
    )
    all_rf = exchange([own_rf] * token_count, "tok")
    all_ls = exchange([own_ls] * token_count, "tok")
    *joined, own_lf, own_rs = lax.optimization_barrier((*all_rf, *all_ls, own_lf, own_rs))
    all_rf, all_ls = joined[:token_count], joined[token_count:]
    all_lf = exchange([own_lf] * token_count, "tok")
    all_rs = exchange([own_rs] * token_count, "tok")

    kept = {}
    zero = jnp.zeros((z.rows, z.block), jnp.bfloat16)
    ticks = z.micro + SKEW * (sections - 1)
    arrivals, sent, adjoint, mids = {}, {}, {}, {}
    wides, acts, derivs, seconds = [], [], [], []
    scalars = []
    for k in range(ticks):
        micro = k - SKEW * depth
        active = jnp.logical_and(micro >= 0, micro < z.micro)
        scalars.append(scalars_of(jnp.where(active, micro, z.micro)))

    def mid_stage(m):
        if m < z.micro:
            pieces = first_mid(z, base, m, inputs, rf_mid)
            mids[m] = exchange(pieces, "hidden")

    def wide_stage(m):
        if m < z.micro:
            wide, act, deriv = forward_wide(z, base, mids.pop(m), lf_mid)
            wides.append(wide)
            acts.append(act)
            derivs.append(deriv)

    def second_stage(m):
        if 0 <= m < z.micro:
            pieces = second_mid(z, base, acts[m], rs_mid)
            seconds.append(exchange(pieces, "hidden"))

    def in_stage(k):
        incoming = arrivals.pop(k, zero)
        kept["gy"], adjoint[k], pieces = backward_in(
            z, scalars[k], k, top_adjoint, incoming, ls_in, kept.get("gy")
        )
        sent[k] = exchange(pieces, "hidden")

    def back_stage(k):
        options = [
            (c, derivs[k - SKEW * c])
            for c in range(sections)
            if 0 <= k - SKEW * c < z.micro
        ]
        kept["gw"], kept["gp"], pieces = backward_wide(
            z, scalars[k], sent[k], rs_back, lf_back, options, kept.get("gw"), kept.get("gp")
        )
        sent[k] = exchange(pieces, "hidden")

    def out_stage(k):
        kept["gn"], kept["adj"], nxt = backward_out(
            z, scalars[k], sent.pop(k), rf_out, adjoint.pop(k), kept.get("gn"), kept.get("adj")
        )
        if k + SKEW < ticks:
            route = [(i, i - 1) for i in range(1, sections)]
            arrivals[k + SKEW] = lax.ppermute(nxt, "section", route)

    rf_mid, rf_out = prepare(z, base, all_rf, ("p", "t"))
    mid_stage(0)
    (ls_in,) = prepare(z, base, all_ls, ("tp",))
    in_stage(0)
    mid_stage(1)
    lf_mid, lf_back = prepare(z, base, all_lf, ("n", "tp"))
    wide_stage(0)
    (rs_back,) = prepare(z, base, all_rs, ("t",))
    back_stage(0)
    mid_stage(2)
    (rs_mid,) = prepare(z, base, all_rs, ("p",))
    wide_stage(1)

    def final(left, right, kind):
        got = gradient(z, base, kept[left], right, kind, 0, z.micro)
        return finish(z, got, shared)

    for k in range(1, ticks):
        in_stage(k)
        if k == ticks - 1:
            grad_ls = final("gy", seconds, "pieces")
        out_stage(k - 1)
        mid_stage(k + 2)
        second_stage(k - (ticks - 1 - z.micro))
        back_stage(k)
        wide_stage(k + 1)
    grad_rs = final("gw", acts, "list")
    grad_lf = final("gp", wides, "list")
    out_stage(ticks - 1)
    grad_rf = final("gn", inputs, "rows")
    adjoints = token_rows(z, base, kept["adj"])
    return adjoints[None], grad_rf, grad_lf, grad_rs, grad_ls


def solution(mesh):
    blocks = P("section", ("hidden", "tok"), None, None)
    rows = P("section", "tok", "hidden")

    def step(*arrays):
        mapped = jax.shard_map(
            on_device,
            mesh=mesh,
            in_specs=(rows, P("tok", "hidden"), blocks, blocks, blocks, blocks),
            out_specs=(rows, blocks, blocks, blocks, blocks),
            check_vma=False,
        )
        return mapped(*arrays)

    return step
```

```python
import math

import jax
import jax.numpy as jnp
from jax import lax
from jax.experimental import pallas as pl
from jax.experimental.pallas import tpu as pltpu
from jax.sharding import PartitionSpec as P


GROUPS = 2
SKEW = 2
UNROLL = 8
SIDE = 4
SEND = 4


gelu_coef = 0.7978845608028654
NT = (((1,), (1,)), ((), ()))
NN = (((1,), (0,)), ((), ()))


def gelu_parts(preact):
    inner_arg = gelu_coef * (preact + 0.044715 * preact * preact * preact)
    squashed = jnp.tanh(inner_arg)
    activation = 0.5 * preact * (1.0 + squashed)
    derivative = 0.5 * (1.0 + squashed) + 0.5 * preact * (1.0 - squashed * squashed) * gelu_coef * (
        1.0 + 3.0 * 0.044715 * preact * preact
    )
    return (activation, derivative)


def dot(a, b, dims=NN):
    return lax.dot_general(a, b, dims, preferred_element_type=jnp.float32)


def partner(me, distance, count):
    if count & (count - 1) == 0:
        return me ^ distance
    return lax.rem(me + distance, count)


def source(me, distance, count):
    if count & (count - 1) == 0:
        return me ^ distance
    return lax.rem(me + count - distance, count)


def exchange(pieces, axis):
    count = len(pieces)
    out = [pieces[0]]
    for distance in range(1, count):
        if count & (count - 1) == 0:
            route = [(i, i ^ distance) for i in range(count)]
        else:
            route = [(i, (i + distance) % count) for i in range(count)]
        out.append(lax.ppermute(pieces[distance], axis, route))
    return out


class Shape:
    def __init__(self, hidden_count, token_count, local_count, block, tok_rows):
        self.hidden = hidden_count
        self.tok = token_count
        self.local = local_count
        self.block = block
        self.groups = GROUPS
        self.pairs = local_count // GROUPS
        self.tokens = block // GROUPS
        self.micro = tok_rows // self.tokens
        self.share = local_count // token_count
        self.rows = self.pairs * block
        self.picked = block // GROUPS
        self.piece = self.pairs * local_count
        self.pitch = local_count + 8
        self.tok_rows = tok_rows
        self.width = local_count * block


def lane_group(z, rows):
    return lax.broadcasted_iota(jnp.int32, (rows, z.block), 1) // z.tokens


def pick(parts, group):
    out = parts[0]
    for g in range(1, len(parts)):
        out = jnp.where(group == g, parts[g], out)
    return out


def spread(z, values):
    turned = [values] + [
        pltpu.roll(values, s * z.tokens, 1) for s in range(1, z.groups)
    ]
    group = lane_group(z, values.shape[0])
    return [
        pick([turned[(q - g) % z.groups] for q in range(z.groups)], group).astype(jnp.bfloat16)
        for g in range(z.groups)
    ]


def produce(z, wire, weight, values, index):
    full = dot(weight, values)
    parts = [full[g * z.picked : (g + 1) * z.picked] for g in range(z.groups)]
    wire[pl.ds(index, z.picked, stride=z.pitch), :] = pick(parts, lane_group(z, z.picked))


def send_pieces(z, wire, hid, piece_refs):
    for d, ref in enumerate(piece_refs):
        first = partner(hid, d, z.hidden) * z.pairs

        def one(pair):
            start = pl.multiple_of((first + pair) * z.pitch, 8)
            at = pl.multiple_of(pair * z.local, z.local)
            ref[pl.ds(at, z.local), :] = wire[pl.ds(start, z.local), :].astype(jnp.bfloat16)

        loop(z.pairs, one, SEND)


def block_rows(z, ref, index):
    return ref[pl.ds(pl.multiple_of(index * z.block, z.block), z.block), :]


def pair_rows(z, pair):
    return pl.ds(pl.multiple_of(pair * z.block, z.block), z.block)


def place(z, piece_refs, hid, pair, ref):
    for d, piece in enumerate(piece_refs):
        src = source(hid, d, z.hidden)
        start = pl.multiple_of(pair * z.block + src * z.local, z.local)
        ref[pl.ds(start, z.local), :] = piece[
            pl.ds(pl.multiple_of(pair * z.local, z.local), z.local), :
        ]


def consume(z, weight_ref, values, pair):
    parts = [dot(block_rows(z, weight_ref, g * z.pairs + pair), values) for g in range(z.groups)]
    return pick(parts, lane_group(z, z.block))


def loop(count, body, unroll=UNROLL):
    def step(i, carry):
        body(i)
        return carry

    lax.fori_loop(0, count, step, 0, unroll=unroll)


def whole(shape):
    return pl.BlockSpec(shape, lambda i, s: tuple(0 for _ in shape))


ANY = pl.BlockSpec(memory_space=pl.ANY)


class Order:
    token = None


def call(
    body, scalars, args, in_specs, outs, out_specs, scratch=(), aliases=None, flops=0, grant=12
):
    size = lambda a: math.prod(a.shape) * a.dtype.itemsize
    moved = sum(size(a) for a, s in zip(args, in_specs) if s is not ANY)
    moved += sum(size(o) for o in outs)
    n_in, n_out = len(args), len(outs)

    def ordered(s, *refs):
        body(s, *refs[:n_in], *refs[n_in + 1 : n_in + 1 + n_out], *refs[n_in + n_out + 2 :])

    token = Order.token
    *got, Order.token = pl.pallas_call(
        ordered,
        grid_spec=pltpu.PrefetchScalarGridSpec(
            num_scalar_prefetch=1,
            grid=(1,),
            in_specs=[*in_specs, ANY],
            out_specs=[*out_specs, ANY],
            scratch_shapes=list(scratch),
        ),
        out_shape=[*outs, jax.ShapeDtypeStruct(token.shape, token.dtype)],
        input_output_aliases={**(aliases or {}), n_in + 1: n_out},
        cost_estimate=pl.CostEstimate(flops=flops, bytes_accessed=moved, transcendentals=0),
        compiler_params=pltpu.CompilerParams(vmem_limit_bytes=grant * 2**20),
    )(scalars, *args, token)
    return got


def bf16(*shape):
    return jax.ShapeDtypeStruct(shape, jnp.bfloat16)


def f32(*shape):
    return jax.ShapeDtypeStruct(shape, jnp.float32)


def shuffle_matrix(z):
    row = lax.broadcasted_iota(jnp.int32, (z.block, z.block), 0)
    col = lax.broadcasted_iota(jnp.int32, (z.block, z.block), 1)
    g = row // z.picked
    rest = row - g * z.picked
    h = rest // z.pairs
    pair = rest - h * z.pairs
    return (col == h * z.local + g * z.pairs + pair).astype(jnp.bfloat16)


def unit_matrix(z):
    row = lax.broadcasted_iota(jnp.int32, (z.block, z.block), 0)
    col = lax.broadcasted_iota(jnp.int32, (z.block, z.block), 1)
    return (col == row).astype(jnp.bfloat16)


def prepare(z, scalars, pieces, forms):
    def body(s, *refs):
        ins, outs = refs[: z.tok], refs[z.tok :]
        unit, shuffle = unit_matrix(z), shuffle_matrix(z)
        for d, piece in enumerate(ins):
            first = source(s[3], d, z.tok) * z.share

            def one(i):
                w = block_rows(z, piece, i)
                at = pair_rows(z, first + i)
                for form, out in zip(forms, outs):
                    if form == "n":
                        out[at, :] = w
                    else:
                        left = shuffle if "p" in form else unit
                        out[at, :] = dot(left, w, NT if "t" in form else NN).astype(jnp.bfloat16)

            loop(z.share, one)

    size = z.local * z.block
    return call(
        body, scalars, pieces,
        [whole((z.share * z.block, z.block))] * z.tok,
        [bf16(size, z.block)] * len(forms), [whole((size, z.block))] * len(forms),
    )


def piece_specs(z):
    return [whole((z.piece, z.block))] * z.hidden


def piece_shapes(z):
    return [bf16(z.piece, z.block)] * z.hidden


def wire_scratch(z):
    return pltpu.VMEM((z.picked * z.pitch, z.block), jnp.float32)


def matmul_flops(z, count):
    return 2 * count * z.local * z.block**3


def first_mid(z, scalars, m, inputs, weight):
    def body(s, x, w, *rest):
        pieces, wire = rest[: z.hidden], rest[z.hidden]

        def one(b):
            cols = pl.ds(pl.multiple_of(b * z.block, z.block), z.block)
            xb = x[:, cols]
            values = jnp.concatenate([xb] * z.groups, axis=0)
            full = dot(block_rows(z, w, b), values, NT)
            parts = [full[g * z.picked : (g + 1) * z.picked] for g in range(z.groups)]
            wire[pl.ds(b, z.picked, stride=z.pitch), :] = pick(parts, lane_group(z, z.picked))

        loop(z.local, one)
        send_pieces(z, wire, s[0], pieces)

    return call(
        body, scalars, [inputs, weight],
        [pl.BlockSpec((z.tokens, z.width), lambda i, s: (m, 0)), whole(weight.shape)],
        piece_shapes(z), piece_specs(z), [wire_scratch(z)], flops=matmul_flops(z, 1),
    )


def forward_wide(z, scalars, pieces, weight):
    def body(s, *refs):
        ins, w = refs[: z.hidden], refs[z.hidden]
        fw, act, deriv = refs[z.hidden + 1 :]

        def one(pair):
            place(z, ins, s[0], pair, fw)
            at = pair_rows(z, pair)
            a, d = gelu_parts(consume(z, w, fw[at, :], pair))
            act[at, :] = a.astype(jnp.bfloat16)
            deriv[at, :] = d.astype(jnp.bfloat16)

        loop(z.pairs, one)

    return call(
        body, scalars, [*pieces, weight],
        piece_specs(z) + [whole(weight.shape)],
        [bf16(z.rows, z.block)] * 3, [whole((z.rows, z.block))] * 3, flops=matmul_flops(z, 1),
    )


def second_mid(z, scalars, act, weight):
    def body(s, a, w, *rest):
        pieces, wire = rest[: z.hidden], rest[z.hidden]

        def one(pair):
            values = a[pair_rows(z, pair), :].astype(jnp.float32)
            for g, repeated in enumerate(spread(z, values)):
                index = g * z.pairs + pair
                produce(z, wire, block_rows(z, w, index), repeated, index)

        loop(z.pairs, one, SIDE)
        send_pieces(z, wire, s[0], pieces)

    return call(
        body, scalars, [act, weight],
        [whole(act.shape), whole(weight.shape)],
        piece_shapes(z), piece_specs(z), [wire_scratch(z)], flops=matmul_flops(z, 1),
    )


def saved_shape(z):
    return bf16(z.micro + 1, z.rows, z.block)


def chained(arrays, first):
    given = [a for a in arrays if a is not None]
    return given, [ANY] * len(given), {first + 1 + i: i for i in range(len(given))}


def saved_spec(z):
    return pl.BlockSpec((1, z.rows, z.block), lambda i, s: (s[2], 0, 0))


def backward_in(z, scalars, k, top, incoming, weight, gy_saved):
    has_top = k < z.micro

    def body(s, *refs):
        if has_top:
            t, inc, w, *rest = refs
        else:
            inc, w, *rest = refs
        rest = rest[len(given) :]
        gy, rest = rest[0], rest[1:]
        if has_top:
            plain, rest = rest[0], rest[1:]
        pieces, wire = rest[: z.hidden], rest[z.hidden]

        if has_top:

            @pl.when(s[1] == 0)
            def _():
                unit = unit_matrix(z)

                def one(pair):
                    parts = []
                    for g in range(z.groups):
                        start = pl.multiple_of((g * z.pairs + pair) * z.block, z.block)
                        parts.append(t[:, pl.ds(start, z.block)])
                    values = jnp.concatenate(parts, axis=0)
                    plain[pair_rows(z, pair), :] = dot(unit, values, NT).astype(jnp.bfloat16)

                loop(z.pairs, one, SIDE)

            @pl.when(s[1] != 0)
            def _():
                plain[...] = inc[...]

            held = plain
        else:
            held = inc

        def one(pair):
            at = pair_rows(z, pair)
            value = held[at, :]
            gy[0, at, :] = value
            for g, repeated in enumerate(spread(z, value.astype(jnp.float32))):
                index = g * z.pairs + pair
                produce(z, wire, block_rows(z, w, index), repeated, index)

        loop(z.pairs, one)
        send_pieces(z, wire, s[0], pieces)

    flat = (z.rows, z.block)
    args = [incoming, weight]
    specs = [whole(flat), whole(weight.shape)]
    if has_top:
        args = [top] + args
        specs = [pl.BlockSpec((z.tokens, z.width), lambda i, s: (k, 0))] + specs
    given, given_specs, aliases = chained([gy_saved], len(args))
    args, specs = args + given, specs + given_specs
    outs = [saved_shape(z)]
    out_specs = [saved_spec(z)]
    if has_top:
        outs.append(bf16(*flat))
        out_specs.append(whole(flat))
    got = call(
        body, scalars, args, specs,
        outs + piece_shapes(z), out_specs + piece_specs(z), [wire_scratch(z)],
        aliases=aliases, flops=matmul_flops(z, 1),
    )
    if has_top:
        return got[0], got[1], got[2:]
    return got[0], incoming, got[1:]


def backward_wide(z, scalars, pieces, weight_rs, weight_lf, options, gw_saved, gp_saved):
    def body(s, *refs):
        ins, refs = refs[: z.hidden], refs[z.hidden :]
        rs, lf, refs = refs[0], refs[1], refs[2:]
        derivs, refs = refs[: len(options)], refs[len(options) + len(given) :]
        gw, gp, refs = refs[0], refs[1], refs[2:]
        out, (wire, deriv, sem) = refs[: z.hidden], refs[z.hidden :]
        if len(options) == 1:
            pltpu.make_async_copy(derivs[0], deriv, sem).start()
        else:
            first, last = options[0][0], options[-1][0]
            for (where, _), ref in zip(options, derivs):
                here = s[1] == where
                if where == first:
                    here = s[1] <= where
                elif where == last:
                    here = s[1] >= where

                @pl.when(here)
                def _():
                    pltpu.make_async_copy(ref, deriv, sem).start()

        loop(z.pairs, lambda pair: place(z, ins, s[0], pair, gw.at[0]), SIDE)
        pltpu.make_async_copy(derivs[0], deriv, sem).wait()

        def one(pair):
            at = pair_rows(z, pair)
            grad = consume(z, rs, gw[0, at, :], pair) * deriv[at, :].astype(jnp.float32)
            rounded = grad.astype(jnp.bfloat16)
            gp[0, at, :] = rounded

        def two(pair):
            values = gp[0, pair_rows(z, pair), :].astype(jnp.float32)
            for g, repeated in enumerate(spread(z, values)):
                index = g * z.pairs + pair
                produce(z, wire, block_rows(z, lf, index), repeated, index)

        loop(z.pairs, one)
        loop(z.pairs, two)
        send_pieces(z, wire, s[0], out)

    args = [*pieces, weight_rs, weight_lf, *[d for _, d in options]]
    given, given_specs, aliases = chained([gw_saved, gp_saved], len(args))
    args += given
    got = call(
        body, scalars, args,
        piece_specs(z) + [whole(weight_rs.shape)] * 2 + [ANY] * len(options) + given_specs,
        [saved_shape(z)] * 2 + piece_shapes(z),
        [saved_spec(z)] * 2 + piece_specs(z),
        [wire_scratch(z), pltpu.VMEM((z.rows, z.block), jnp.bfloat16), pltpu.SemaphoreType.DMA],
        aliases=aliases, flops=matmul_flops(z, 2),
    )
    return got[0], got[1], got[2:]


def backward_out(z, scalars, pieces, weight, gy, gn_saved, adj_saved):
    def body(s, *refs):
        ins, (w, g_ref, *rest) = refs[: z.hidden], refs[z.hidden :]
        gn, adj, nxt = rest[len(given) :]

        def one(pair):
            at = pair_rows(z, pair)
            place(z, ins, s[0], pair, gn.at[0])
            grad = consume(z, w, gn[0, at, :], pair)
            value = (g_ref[at, :].astype(jnp.float32) + grad).astype(jnp.bfloat16)
            adj[0, at, :] = value
            nxt[at, :] = value

        loop(z.pairs, one)

    args = [*pieces, weight, gy]
    given, given_specs, aliases = chained([gn_saved, adj_saved], len(args))
    args += given
    flat = (z.rows, z.block)
    return call(
        body, scalars, args,
        piece_specs(z) + [whole(weight.shape), whole(flat), *given_specs],
        [saved_shape(z)] * 2 + [bf16(*flat)],
        [saved_spec(z)] * 2 + [whole(flat)],
        aliases=aliases, flops=matmul_flops(z, 1),
    )


def all_saved(z):
    return pl.BlockSpec((z.micro, z.rows, z.block), lambda i, s: (0, 0, 0))


def join_pieces(z, scalars, groups):
    pieces = [p for group in groups for p in group]

    def body(s, *refs):
        ins, out = refs[:-1], refs[-1]
        for m in range(z.micro):
            group = ins[m * z.hidden : (m + 1) * z.hidden]
            loop(z.pairs, lambda pair: place(z, group, s[0], pair, out.at[m]), 4)

    shape = (z.micro, z.rows, z.block)
    return call(
        body, scalars, pieces, [whole(p.shape) for p in pieces],
        [bf16(*shape)], [whole(shape)],
    )[0]


def gradient(z, scalars, left, right, kind, distances, unroll=2):
    right_args = list(right) if kind == "list" else [right]
    count = z.share * z.block

    def body(s, l, *refs):
        ins, outs = refs[: len(right_args)], refs[len(right_args) :]
        group_of = lane_group(z, z.block)
        for d, out in zip(distances, outs):
            owner = partner(s[3], d, z.tok) * z.share

            def one(i):
                index = owner + i
                g = lax.div(index, z.pairs)
                pair = index - g * z.pairs
                at = pair_rows(z, pair)
                total = None
                for m in range(z.micro):
                    a = l[m, at, :]
                    a = jnp.where(group_of == g, a, jnp.zeros_like(a))
                    if kind == "rows":
                        rows = []
                        for q in range(z.groups):
                            start = pl.multiple_of((q * z.pairs + pair) * z.block, z.block)
                            first = m * z.tokens
                            rows.append(ins[0][first : first + z.tokens, pl.ds(start, z.block)])
                        term = dot(a, jnp.concatenate(rows, axis=0))
                    else:
                        b = ins[0][m, at, :] if kind == "saved" else ins[m][at, :]
                        term = dot(a, b, NT)
                    total = term if total is None else total + term
                out[pair_rows(z, i), :] = total.astype(out.dtype)

            loop(z.share, one, unroll)

    args = [left, *right_args]
    specs = [all_saved(z)] + [whole(a.shape) for a in right_args]
    outs = [f32(count, z.block) if d == 0 else bf16(count, z.block) for d in distances]
    return call(
        body, scalars, args, specs, outs, [whole((count, z.block))] * len(outs),
        flops=matmul_flops(z, z.micro), grant=28,
    )


def finish(z, received, shared):
    total = received[0]
    for other in received[1:]:
        total = total + other.astype(jnp.float32)
    return (total * shared).reshape(1, z.share, z.block, z.block)


def token_rows(z, scalars, saved):
    def body(s, a, out):
        for m in range(z.micro):

            def one(pair):
                turned = a[m, pair_rows(z, pair), :].astype(jnp.float32).T.astype(jnp.bfloat16)
                for g in range(z.groups):
                    start = pl.multiple_of((g * z.pairs + pair) * z.block, z.block)
                    out[m * z.tokens : (m + 1) * z.tokens, pl.ds(start, z.block)] = turned[
                        g * z.tokens : (g + 1) * z.tokens
                    ]

            loop(z.pairs, one, 2)

    return call(
        body, scalars, [saved], [all_saved(z)],
        [bf16(z.tok_rows, z.width)], [whole((z.tok_rows, z.width))], grant=28,
    )[0]


def on_device(section_inputs, top_adjoint, right_first, left_first, right_second, left_second):
    sections = lax.axis_size("section")
    token_count = lax.axis_size("tok")
    hidden_count = lax.axis_size("hidden")
    _, share, block, _ = right_first.shape
    inputs = section_inputs[0]
    tok_rows = inputs.shape[0]
    z = Shape(hidden_count, token_count, share * token_count, block, tok_rows)
    hid = lax.axis_index("hidden")
    depth = sections - 1 - lax.axis_index("section")
    tok = lax.axis_index("tok")
    shared = 1.0 / math.sqrt(tok_rows * token_count)

    def scalars_of(slot):
        return jnp.stack([hid, depth, slot, tok]).astype(jnp.int32)

    base = scalars_of(jnp.int32(0))

    Order.token = jnp.zeros((8, 128), jnp.float32)
    own_rf, own_lf, own_rs, own_ls = (
        w.reshape(share * block, block)
        for w in (right_first, left_first, right_second, left_second)
    )
    all_rf = exchange([own_rf] * token_count, "tok")
    all_ls = exchange([own_ls] * token_count, "tok")
    *joined, own_lf, own_rs = lax.optimization_barrier((*all_rf, *all_ls, own_lf, own_rs))
    all_rf, all_ls = joined[:token_count], joined[token_count:]
    all_lf = exchange([own_lf] * token_count, "tok")
    all_rs = exchange([own_rs] * token_count, "tok")

    kept = {}
    zero = jnp.zeros((z.rows, z.block), jnp.bfloat16)
    ticks = z.micro + SKEW * (sections - 1)
    arrivals, sent, adjoint, mids = {}, {}, {}, {}
    wides, acts, derivs, seconds = [], [], [], []
    scalars = []
    for k in range(ticks):
        micro = k - SKEW * depth
        active = jnp.logical_and(micro >= 0, micro < z.micro)
        scalars.append(scalars_of(jnp.where(active, micro, z.micro)))

    def mid_stage(m):
        if m < z.micro:
            pieces = first_mid(z, base, m, inputs, rf_mid)
            mids[m] = exchange(pieces, "hidden")

    def wide_stage(m):
        if m < z.micro:
            wide, act, deriv = forward_wide(z, base, mids.pop(m), lf_mid)
            wides.append(wide)
            acts.append(act)
            derivs.append(deriv)

    def second_stage(m):
        if 0 <= m < z.micro:
            pieces = second_mid(z, base, acts[m], rs_mid)
            seconds.append(exchange(pieces, "hidden"))

    def in_stage(k):
        incoming = arrivals.pop(k, zero)
        kept["gy"], adjoint[k], pieces = backward_in(
            z, scalars[k], k, top_adjoint, incoming, ls_in, kept.get("gy")
        )
        sent[k] = exchange(pieces, "hidden")

    def back_stage(k):
        options = [
            (c, derivs[k - SKEW * c])
            for c in range(sections)
            if 0 <= k - SKEW * c < z.micro
        ]
        kept["gw"], kept["gp"], pieces = backward_wide(
            z, scalars[k], sent[k], rs_back, lf_back, options, kept.get("gw"), kept.get("gp")
        )
        sent[k] = exchange(pieces, "hidden")

    def out_stage(k):
        kept["gn"], kept["adj"], nxt = backward_out(
            z, scalars[k], sent.pop(k), rf_out, adjoint.pop(k), kept.get("gn"), kept.get("adj")
        )
        if k + SKEW < ticks:
            route = [(i, i - 1) for i in range(1, sections)]
            arrivals[k + SKEW] = lax.ppermute(nxt, "section", route)

    rf_mid, rf_out = prepare(z, base, all_rf, ("p", "t"))
    mid_stage(0)
    (ls_in,) = prepare(z, base, all_ls, ("tp",))
    in_stage(0)
    mid_stage(1)
    lf_mid, lf_back = prepare(z, base, all_lf, ("n", "tp"))
    wide_stage(0)
    (rs_back,) = prepare(z, base, all_rs, ("t",))
    back_stage(0)
    mid_stage(2)
    (rs_mid,) = prepare(z, base, all_rs, ("p",))
    wide_stage(1)
    everyone, others = list(range(token_count)), list(range(1, token_count))

    def final(left, right, kind, unroll=SIDE):
        got = gradient(z, base, kept[left], right, kind, everyone, unroll)
        return finish(z, exchange(got, "tok"), shared)

    for k in range(1, ticks):
        in_stage(k)
        if k == ticks - 1:
            sent_ls = gradient(z, base, kept["gy"], joined_ls, "saved", others, 4)
            sent_ls = exchange([None, *sent_ls], "tok")
        out_stage(k - 1)
        mid_stage(k + 2)
        second_stage(k - (ticks - 1 - z.micro))
        back_stage(k)
        wide_stage(k + 1)
        if k == ticks - 2:
            joined_ls = join_pieces(z, base, seconds)
    grad_rs = final("gw", acts, "list")
    grad_lf = final("gp", wides, "list")
    out_stage(ticks - 1)
    grad_rf = final("gn", inputs, "rows", 2)
    own_part = gradient(z, base, kept["gy"], joined_ls, "saved", [0])
    grad_ls = finish(z, [own_part[0], *sent_ls[1:]], shared)
    adjoints = token_rows(z, base, kept["adj"])
    return adjoints[None], grad_rf, grad_lf, grad_rs, grad_ls


def solution(mesh):
    blocks = P("section", ("hidden", "tok"), None, None)
    rows = P("section", "tok", "hidden")

    def step(*arrays):
        mapped = jax.shard_map(
            on_device,
            mesh=mesh,
            in_specs=(rows, P("tok", "hidden"), blocks, blocks, blocks, blocks),
            out_specs=(rows, blocks, blocks, blocks, blocks),
            check_vma=False,
        )
        return mapped(*arrays)

    return step
```

```python
import math

import jax
import jax.numpy as jnp
from jax import lax
from jax.experimental import pallas as pl
from jax.experimental.pallas import tpu as pltpu
from jax.sharding import PartitionSpec as P


GROUPS = 2
SKEW = 2
UNROLL = 8
SIDE = 4
SEND = 4


gelu_coef = 0.7978845608028654
NT = (((1,), (1,)), ((), ()))
NN = (((1,), (0,)), ((), ()))


def gelu_parts(preact):
    inner_arg = gelu_coef * (preact + 0.044715 * preact * preact * preact)
    squashed = jnp.tanh(inner_arg)
    activation = 0.5 * preact * (1.0 + squashed)
    derivative = 0.5 * (1.0 + squashed) + 0.5 * preact * (1.0 - squashed * squashed) * gelu_coef * (
        1.0 + 3.0 * 0.044715 * preact * preact
    )
    return (activation, derivative)


def dot(a, b, dims=NN):
    return lax.dot_general(a, b, dims, preferred_element_type=jnp.float32)


def partner(me, distance, count):
    if count & (count - 1) == 0:
        return me ^ distance
    return lax.rem(me + distance, count)


def source(me, distance, count):
    if count & (count - 1) == 0:
        return me ^ distance
    return lax.rem(me + count - distance, count)


def exchange(pieces, axis):
    count = len(pieces)
    out = [pieces[0]]
    for distance in range(1, count):
        if count & (count - 1) == 0:
            route = [(i, i ^ distance) for i in range(count)]
        else:
            route = [(i, (i + distance) % count) for i in range(count)]
        out.append(lax.ppermute(pieces[distance], axis, route))
    return out


class Shape:
    def __init__(self, hidden_count, token_count, local_count, block, tok_rows):
        self.hidden = hidden_count
        self.tok = token_count
        self.local = local_count
        self.block = block
        self.groups = GROUPS
        self.pairs = local_count // GROUPS
        self.tokens = block // GROUPS
        self.micro = tok_rows // self.tokens
        self.share = local_count // token_count
        self.rows = self.pairs * block
        self.picked = block // GROUPS
        self.piece = self.pairs * local_count
        self.pitch = local_count + 8
        self.tok_rows = tok_rows
        self.width = local_count * block


def lane_group(z, rows):
    return lax.broadcasted_iota(jnp.int32, (rows, z.block), 1) // z.tokens


def pick(parts, group):
    out = parts[0]
    for g in range(1, len(parts)):
        out = jnp.where(group == g, parts[g], out)
    return out


def spread(z, values):
    turned = [values] + [
        pltpu.roll(values, s * z.tokens, 1) for s in range(1, z.groups)
    ]
    group = lane_group(z, values.shape[0])
    return [
        pick([turned[(q - g) % z.groups] for q in range(z.groups)], group).astype(jnp.bfloat16)
        for g in range(z.groups)
    ]


def produce(z, wire, weight, values, index):
    full = dot(weight, values)
    parts = [full[g * z.picked : (g + 1) * z.picked] for g in range(z.groups)]
    wire[pl.ds(index, z.picked, stride=z.pitch), :] = pick(parts, lane_group(z, z.picked))


def send_pieces(z, wire, hid, piece_refs):
    for d, ref in enumerate(piece_refs):
        first = partner(hid, d, z.hidden) * z.pairs

        def one(pair):
            start = pl.multiple_of((first + pair) * z.pitch, 8)
            at = pl.multiple_of(pair * z.local, z.local)
            ref[pl.ds(at, z.local), :] = wire[pl.ds(start, z.local), :].astype(jnp.bfloat16)

        loop(z.pairs, one, SEND)


def block_rows(z, ref, index):
    return ref[pl.ds(pl.multiple_of(index * z.block, z.block), z.block), :]


def pair_rows(z, pair):
    return pl.ds(pl.multiple_of(pair * z.block, z.block), z.block)


def place(z, piece_refs, hid, pair, ref):
    for d, piece in enumerate(piece_refs):
        src = source(hid, d, z.hidden)
        start = pl.multiple_of(pair * z.block + src * z.local, z.local)
        ref[pl.ds(start, z.local), :] = piece[
            pl.ds(pl.multiple_of(pair * z.local, z.local), z.local), :
        ]


def consume(z, weight_ref, values, pair):
    parts = [dot(block_rows(z, weight_ref, g * z.pairs + pair), values) for g in range(z.groups)]
    return pick(parts, lane_group(z, z.block))


def loop(count, body, unroll=UNROLL):
    def step(i, carry):
        body(i)
        return carry

    lax.fori_loop(0, count, step, 0, unroll=unroll)


def whole(shape):
    return pl.BlockSpec(shape, lambda i, s: tuple(0 for _ in shape))


ANY = pl.BlockSpec(memory_space=pl.ANY)


class Order:
    token = None


def call(
    body, scalars, args, in_specs, outs, out_specs, scratch=(), aliases=None, flops=0, grant=12
):
    size = lambda a: math.prod(a.shape) * a.dtype.itemsize
    moved = sum(size(a) for a, s in zip(args, in_specs) if s is not ANY)
    moved += sum(size(o) for o in outs)
    n_in, n_out = len(args), len(outs)

    def ordered(s, *refs):
        body(s, *refs[:n_in], *refs[n_in + 1 : n_in + 1 + n_out], *refs[n_in + n_out + 2 :])

    token = Order.token
    *got, Order.token = pl.pallas_call(
        ordered,
        grid_spec=pltpu.PrefetchScalarGridSpec(
            num_scalar_prefetch=1,
            grid=(1,),
            in_specs=[*in_specs, ANY],
            out_specs=[*out_specs, ANY],
            scratch_shapes=list(scratch),
        ),
        out_shape=[*outs, jax.ShapeDtypeStruct(token.shape, token.dtype)],
        input_output_aliases={**(aliases or {}), n_in + 1: n_out},
        cost_estimate=pl.CostEstimate(flops=flops, bytes_accessed=moved, transcendentals=0),
        compiler_params=pltpu.CompilerParams(vmem_limit_bytes=grant * 2**20),
    )(scalars, *args, token)
    return got


def bf16(*shape):
    return jax.ShapeDtypeStruct(shape, jnp.bfloat16)


def f32(*shape):
    return jax.ShapeDtypeStruct(shape, jnp.float32)


def shuffle_matrix(z):
    row = lax.broadcasted_iota(jnp.int32, (z.block, z.block), 0)
    col = lax.broadcasted_iota(jnp.int32, (z.block, z.block), 1)
    g = row // z.picked
    rest = row - g * z.picked
    h = rest // z.pairs
    pair = rest - h * z.pairs
    return (col == h * z.local + g * z.pairs + pair).astype(jnp.bfloat16)


def unit_matrix(z):
    row = lax.broadcasted_iota(jnp.int32, (z.block, z.block), 0)
    col = lax.broadcasted_iota(jnp.int32, (z.block, z.block), 1)
    return (col == row).astype(jnp.bfloat16)


def prepare(z, scalars, pieces, forms):
    def body(s, *refs):
        ins, outs = refs[: z.tok], refs[z.tok :]
        unit, shuffle = unit_matrix(z), shuffle_matrix(z)
        for d, piece in enumerate(ins):
            first = source(s[3], d, z.tok) * z.share

            def one(i):
                w = block_rows(z, piece, i)
                at = pair_rows(z, first + i)
                for form, out in zip(forms, outs):
                    if form == "n":
                        out[at, :] = w
                    else:
                        left = shuffle if "p" in form else unit
                        out[at, :] = dot(left, w, NT if "t" in form else NN).astype(jnp.bfloat16)

            loop(z.share, one)

    size = z.local * z.block
    return call(
        body, scalars, pieces,
        [whole((z.share * z.block, z.block))] * z.tok,
        [bf16(size, z.block)] * len(forms), [whole((size, z.block))] * len(forms),
    )


def piece_specs(z):
    return [whole((z.piece, z.block))] * z.hidden


def piece_shapes(z):
    return [bf16(z.piece, z.block)] * z.hidden


def wire_scratch(z):
    return pltpu.VMEM((z.picked * z.pitch, z.block), jnp.float32)


def matmul_flops(z, count):
    return 2 * count * z.local * z.block**3


def first_mid(z, scalars, m, inputs, weight):
    def body(s, x, w, *rest):
        pieces, wire = rest[: z.hidden], rest[z.hidden]

        def one(b):
            cols = pl.ds(pl.multiple_of(b * z.block, z.block), z.block)
            xb = x[:, cols]
            values = jnp.concatenate([xb] * z.groups, axis=0)
            full = dot(block_rows(z, w, b), values, NT)
            parts = [full[g * z.picked : (g + 1) * z.picked] for g in range(z.groups)]
            wire[pl.ds(b, z.picked, stride=z.pitch), :] = pick(parts, lane_group(z, z.picked))

        loop(z.local, one)
        send_pieces(z, wire, s[0], pieces)

    return call(
        body, scalars, [inputs, weight],
        [pl.BlockSpec((z.tokens, z.width), lambda i, s: (m, 0)), whole(weight.shape)],
        piece_shapes(z), piece_specs(z), [wire_scratch(z)], flops=matmul_flops(z, 1),
    )


def forward_wide(z, scalars, pieces, weight):
    def body(s, *refs):
        ins, w = refs[: z.hidden], refs[z.hidden]
        fw, act, deriv = refs[z.hidden + 1 :]

        def one(pair):
            place(z, ins, s[0], pair, fw)
            at = pair_rows(z, pair)
            a, d = gelu_parts(consume(z, w, fw[at, :], pair))
            act[at, :] = a.astype(jnp.bfloat16)
            deriv[at, :] = d.astype(jnp.bfloat16)

        loop(z.pairs, one, SIDE)

    return call(
        body, scalars, [*pieces, weight],
        piece_specs(z) + [whole(weight.shape)],
        [bf16(z.rows, z.block)] * 3, [whole((z.rows, z.block))] * 3, flops=matmul_flops(z, 1),
    )


def second_mid(z, scalars, act, weight):
    def body(s, a, w, *rest):
        pieces, wire = rest[: z.hidden], rest[z.hidden]

        def one(pair):
            values = a[pair_rows(z, pair), :].astype(jnp.float32)
            for g, repeated in enumerate(spread(z, values)):
                index = g * z.pairs + pair
                produce(z, wire, block_rows(z, w, index), repeated, index)

        loop(z.pairs, one, 2)
        send_pieces(z, wire, s[0], pieces)

    return call(
        body, scalars, [act, weight],
        [whole(act.shape), whole(weight.shape)],
        piece_shapes(z), piece_specs(z), [wire_scratch(z)], flops=matmul_flops(z, 1),
    )


def saved_shape(z):
    return bf16(z.micro + 1, z.rows, z.block)


def chained(arrays, first):
    given = [a for a in arrays if a is not None]
    return given, [ANY] * len(given), {first + 1 + i: i for i in range(len(given))}


def saved_spec(z):
    return pl.BlockSpec((1, z.rows, z.block), lambda i, s: (s[2], 0, 0))


def backward_in(z, scalars, k, top, incoming, weight, gy_saved):
    has_top = k < z.micro

    def body(s, *refs):
        if has_top:
            t, inc, w, *rest = refs
        else:
            inc, w, *rest = refs
        rest = rest[len(given) :]
        gy, rest = rest[0], rest[1:]
        if has_top:
            plain, rest = rest[0], rest[1:]
        pieces, wire = rest[: z.hidden], rest[z.hidden]

        if has_top:

            @pl.when(s[1] == 0)
            def _():
                unit = unit_matrix(z)

                def one(pair):
                    parts = []
                    for g in range(z.groups):
                        start = pl.multiple_of((g * z.pairs + pair) * z.block, z.block)
                        parts.append(t[:, pl.ds(start, z.block)])
                    values = jnp.concatenate(parts, axis=0)
                    plain[pair_rows(z, pair), :] = dot(unit, values, NT).astype(jnp.bfloat16)

                loop(z.pairs, one, SIDE)

            @pl.when(s[1] != 0)
            def _():
                plain[...] = inc[...]

            held = plain
        else:
            held = inc

        def one(pair):
            at = pair_rows(z, pair)
            value = held[at, :]
            gy[0, at, :] = value
            for g, repeated in enumerate(spread(z, value.astype(jnp.float32))):
                index = g * z.pairs + pair
                produce(z, wire, block_rows(z, w, index), repeated, index)

        loop(z.pairs, one)
        send_pieces(z, wire, s[0], pieces)

    flat = (z.rows, z.block)
    args = [incoming, weight]
    specs = [whole(flat), whole(weight.shape)]
    if has_top:
        args = [top] + args
        specs = [pl.BlockSpec((z.tokens, z.width), lambda i, s: (k, 0))] + specs
    given, given_specs, aliases = chained([gy_saved], len(args))
    args, specs = args + given, specs + given_specs
    outs = [saved_shape(z)]
    out_specs = [saved_spec(z)]
    if has_top:
        outs.append(bf16(*flat))
        out_specs.append(whole(flat))
    got = call(
        body, scalars, args, specs,
        outs + piece_shapes(z), out_specs + piece_specs(z), [wire_scratch(z)],
        aliases=aliases, flops=matmul_flops(z, 1),
    )
    if has_top:
        return got[0], got[1], got[2:]
    return got[0], incoming, got[1:]


def backward_wide(z, scalars, pieces, weight_rs, weight_lf, options, gw_saved, gp_saved):
    def body(s, *refs):
        ins, refs = refs[: z.hidden], refs[z.hidden :]
        rs, lf, refs = refs[0], refs[1], refs[2:]
        derivs, refs = refs[: len(options)], refs[len(options) + len(given) :]
        gw, gp, refs = refs[0], refs[1], refs[2:]
        out, (wire, deriv, sem) = refs[: z.hidden], refs[z.hidden :]
        if len(options) == 1:
            pltpu.make_async_copy(derivs[0], deriv, sem).start()
        else:
            first, last = options[0][0], options[-1][0]
            for (where, _), ref in zip(options, derivs):
                here = s[1] == where
                if where == first:
                    here = s[1] <= where
                elif where == last:
                    here = s[1] >= where

                @pl.when(here)
                def _():
                    pltpu.make_async_copy(ref, deriv, sem).start()

        loop(z.pairs, lambda pair: place(z, ins, s[0], pair, gw.at[0]), 2)
        pltpu.make_async_copy(derivs[0], deriv, sem).wait()

        def one(pair):
            at = pair_rows(z, pair)
            grad = consume(z, rs, gw[0, at, :], pair) * deriv[at, :].astype(jnp.float32)
            rounded = grad.astype(jnp.bfloat16)
            gp[0, at, :] = rounded

        def two(pair):
            values = gp[0, pair_rows(z, pair), :].astype(jnp.float32)
            for g, repeated in enumerate(spread(z, values)):
                index = g * z.pairs + pair
                produce(z, wire, block_rows(z, lf, index), repeated, index)

        loop(z.pairs, one)
        loop(z.pairs, two)
        send_pieces(z, wire, s[0], out)

    args = [*pieces, weight_rs, weight_lf, *[d for _, d in options]]
    given, given_specs, aliases = chained([gw_saved, gp_saved], len(args))
    args += given
    got = call(
        body, scalars, args,
        piece_specs(z) + [whole(weight_rs.shape)] * 2 + [ANY] * len(options) + given_specs,
        [saved_shape(z)] * 2 + piece_shapes(z),
        [saved_spec(z)] * 2 + piece_specs(z),
        [wire_scratch(z), pltpu.VMEM((z.rows, z.block), jnp.bfloat16), pltpu.SemaphoreType.DMA],
        aliases=aliases, flops=matmul_flops(z, 2),
    )
    return got[0], got[1], got[2:]


def backward_out(z, scalars, pieces, weight, gy, gn_saved, adj_saved):
    def body(s, *refs):
        ins, (w, g_ref, *rest) = refs[: z.hidden], refs[z.hidden :]
        gn, adj, nxt = rest[len(given) :]

        def one(pair):
            at = pair_rows(z, pair)
            place(z, ins, s[0], pair, gn.at[0])
            grad = consume(z, w, gn[0, at, :], pair)
            value = (g_ref[at, :].astype(jnp.float32) + grad).astype(jnp.bfloat16)
            adj[0, at, :] = value
            nxt[at, :] = value

        loop(z.pairs, one, SIDE)

    args = [*pieces, weight, gy]
    given, given_specs, aliases = chained([gn_saved, adj_saved], len(args))
    args += given
    flat = (z.rows, z.block)
    return call(
        body, scalars, args,
        piece_specs(z) + [whole(weight.shape), whole(flat), *given_specs],
        [saved_shape(z)] * 2 + [bf16(*flat)],
        [saved_spec(z)] * 2 + [whole(flat)],
        aliases=aliases, flops=matmul_flops(z, 1),
    )


def all_saved(z):
    return pl.BlockSpec((z.micro, z.rows, z.block), lambda i, s: (0, 0, 0))


def join_pieces(z, scalars, groups):
    pieces = [p for group in groups for p in group]

    def body(s, *refs):
        ins, out = refs[:-1], refs[-1]
        for m in range(z.micro):
            group = ins[m * z.hidden : (m + 1) * z.hidden]
            loop(z.pairs, lambda pair: place(z, group, s[0], pair, out.at[m]), 1)

    shape = (z.micro, z.rows, z.block)
    return call(
        body, scalars, pieces, [whole(p.shape) for p in pieces],
        [bf16(*shape)], [whole(shape)],
    )[0]


def gradient(z, scalars, left, right, kind, distances, unroll=2):
    right_args = list(right) if kind == "list" else [right]
    count = z.share * z.block

    def body(s, l, *refs):
        ins, outs = refs[: len(right_args)], refs[len(right_args) :]
        group_of = lane_group(z, z.block)
        for d, out in zip(distances, outs):
            owner = partner(s[3], d, z.tok) * z.share

            def one(i):
                index = owner + i
                g = lax.div(index, z.pairs)
                pair = index - g * z.pairs
                at = pair_rows(z, pair)
                total = None
                for m in range(z.micro):
                    a = l[m, at, :]
                    a = jnp.where(group_of == g, a, jnp.zeros_like(a))
                    if kind == "rows":
                        rows = []
                        for q in range(z.groups):
                            start = pl.multiple_of((q * z.pairs + pair) * z.block, z.block)
                            first = m * z.tokens
                            rows.append(ins[0][first : first + z.tokens, pl.ds(start, z.block)])
                        term = dot(a, jnp.concatenate(rows, axis=0))
                    else:
                        b = ins[0][m, at, :] if kind == "saved" else ins[m][at, :]
                        term = dot(a, b, NT)
                    total = term if total is None else total + term
                out[pair_rows(z, i), :] = total.astype(out.dtype)

            loop(z.share, one, unroll)

    args = [left, *right_args]
    specs = [all_saved(z)] + [whole(a.shape) for a in right_args]
    outs = [f32(count, z.block) if d == 0 else bf16(count, z.block) for d in distances]
    return call(
        body, scalars, args, specs, outs, [whole((count, z.block))] * len(outs),
        flops=matmul_flops(z, z.micro), grant=28,
    )


def finish(z, received, shared):
    total = received[0]
    for other in received[1:]:
        total = total + other.astype(jnp.float32)
    return (total * shared).reshape(1, z.share, z.block, z.block)


def token_rows(z, scalars, saved):
    def body(s, a, out):
        for m in range(z.micro):

            def one(pair):
                turned = a[m, pair_rows(z, pair), :].astype(jnp.float32).T.astype(jnp.bfloat16)
                for g in range(z.groups):
                    start = pl.multiple_of((g * z.pairs + pair) * z.block, z.block)
                    out[m * z.tokens : (m + 1) * z.tokens, pl.ds(start, z.block)] = turned[
                        g * z.tokens : (g + 1) * z.tokens
                    ]

            loop(z.pairs, one, 1)

    return call(
        body, scalars, [saved], [all_saved(z)],
        [bf16(z.tok_rows, z.width)], [whole((z.tok_rows, z.width))], grant=28,
    )[0]


def on_device(section_inputs, top_adjoint, right_first, left_first, right_second, left_second):
    sections = lax.axis_size("section")
    token_count = lax.axis_size("tok")
    hidden_count = lax.axis_size("hidden")
    _, share, block, _ = right_first.shape
    inputs = section_inputs[0]
    tok_rows = inputs.shape[0]
    z = Shape(hidden_count, token_count, share * token_count, block, tok_rows)
    hid = lax.axis_index("hidden")
    depth = sections - 1 - lax.axis_index("section")
    tok = lax.axis_index("tok")
    shared = 1.0 / math.sqrt(tok_rows * token_count)

    def scalars_of(slot):
        return jnp.stack([hid, depth, slot, tok]).astype(jnp.int32)

    base = scalars_of(jnp.int32(0))

    Order.token = jnp.zeros((8, 128), jnp.float32)
    own_rf, own_lf, own_rs, own_ls = (
        w.reshape(share * block, block)
        for w in (right_first, left_first, right_second, left_second)
    )
    all_rf = exchange([own_rf] * token_count, "tok")
    all_ls = exchange([own_ls] * token_count, "tok")
    *joined, own_lf, own_rs = lax.optimization_barrier((*all_rf, *all_ls, own_lf, own_rs))
    all_rf, all_ls = joined[:token_count], joined[token_count:]
    all_lf = exchange([own_lf] * token_count, "tok")
    all_rs = exchange([own_rs] * token_count, "tok")

    kept = {}
    zero = jnp.zeros((z.rows, z.block), jnp.bfloat16)
    ticks = z.micro + SKEW * (sections - 1)
    arrivals, sent, adjoint, mids = {}, {}, {}, {}
    wides, acts, derivs, seconds = [], [], [], []
    scalars = []
    for k in range(ticks):
        micro = k - SKEW * depth
        active = jnp.logical_and(micro >= 0, micro < z.micro)
        scalars.append(scalars_of(jnp.where(active, micro, z.micro)))

    def mid_stage(m):
        if m < z.micro:
            pieces = first_mid(z, base, m, inputs, rf_mid)
            mids[m] = exchange(pieces, "hidden")

    def wide_stage(m):
        if m < z.micro:
            wide, act, deriv = forward_wide(z, base, mids.pop(m), lf_mid)
            wides.append(wide)
            acts.append(act)
            derivs.append(deriv)

    def second_stage(m):
        if 0 <= m < z.micro:
            pieces = second_mid(z, base, acts[m], rs_mid)
            seconds.append(exchange(pieces, "hidden"))

    def in_stage(k):
        incoming = arrivals.pop(k, zero)
        kept["gy"], adjoint[k], pieces = backward_in(
            z, scalars[k], k, top_adjoint, incoming, ls_in, kept.get("gy")
        )
        sent[k] = exchange(pieces, "hidden")

    def back_stage(k):
        options = [
            (c, derivs[k - SKEW * c])
            for c in range(sections)
            if 0 <= k - SKEW * c < z.micro
        ]
        kept["gw"], kept["gp"], pieces = backward_wide(
            z, scalars[k], sent[k], rs_back, lf_back, options, kept.get("gw"), kept.get("gp")
        )
        sent[k] = exchange(pieces, "hidden")

    def out_stage(k):
        kept["gn"], kept["adj"], nxt = backward_out(
            z, scalars[k], sent.pop(k), rf_out, adjoint.pop(k), kept.get("gn"), kept.get("adj")
        )
        if k + SKEW < ticks:
            route = [(i, i - 1) for i in range(1, sections)]
            arrivals[k + SKEW] = lax.ppermute(nxt, "section", route)

    rf_mid, rf_out = prepare(z, base, all_rf, ("p", "t"))
    mid_stage(0)
    (ls_in,) = prepare(z, base, all_ls, ("tp",))
    in_stage(0)
    mid_stage(1)
    lf_mid, lf_back = prepare(z, base, all_lf, ("n", "tp"))
    wide_stage(0)
    (rs_back,) = prepare(z, base, all_rs, ("t",))
    back_stage(0)
    mid_stage(2)
    (rs_mid,) = prepare(z, base, all_rs, ("p",))
    wide_stage(1)
    everyone, others = list(range(token_count)), list(range(1, token_count))

    def final(left, right, kind, unroll=2):
        got = gradient(z, base, kept[left], right, kind, everyone, unroll)
        return finish(z, exchange(got, "tok"), shared)

    for k in range(1, ticks):
        in_stage(k)
        if k == ticks - 1:
            sent_ls = gradient(z, base, kept["gy"], joined_ls, "saved", others, 4)
            sent_ls = exchange([None, *sent_ls], "tok")
        out_stage(k - 1)
        mid_stage(k + 2)
        second_stage(k - (ticks - 1 - z.micro))
        back_stage(k)
        wide_stage(k + 1)
        if k == ticks - 2:
            joined_ls = join_pieces(z, base, seconds)
    grad_rs = final("gw", acts, "list")
    grad_lf = final("gp", wides, "list")
    out_stage(ticks - 1)
    grad_rf = final("gn", inputs, "rows", 1)
    own_part = gradient(z, base, kept["gy"], joined_ls, "saved", [0], 1)
    grad_ls = finish(z, [own_part[0], *sent_ls[1:]], shared)
    adjoints = token_rows(z, base, kept["adj"])
    return adjoints[None], grad_rf, grad_lf, grad_rs, grad_ls


def solution(mesh):
    blocks = P("section", ("hidden", "tok"), None, None)
    rows = P("section", "tok", "hidden")

    def step(*arrays):
        mapped = jax.shard_map(
            on_device,
            mesh=mesh,
            in_specs=(rows, P("tok", "hidden"), blocks, blocks, blocks, blocks),
            out_specs=(rows, blocks, blocks, blocks, blocks),
            check_vma=False,
        )
        return mapped(*arrays)

    return step
```
